32 devices in a mesh: dp: 8 (over z, y), tensor: 4 (over x, core).
Axes of the slice: x: 2, y: 2, z: 4, core: 2. Of those that a mesh axis runs over, the one named last changes fastest.
Arguments:
- tokens: bfloat16 [16, 2048, 768], P('dp', 'tensor'), may hold values from -6 to 6
- segment_ids: int32 [16, 2048], P('dp'), may hold values from 0 to 11, never falling along the last dimension, each value on 1 to 1024 neighbouring positions
- w_query: bfloat16 [768, 768], P('dp', 'tensor'), may hold values from -0.21875 to 0.21875
- w_key: bfloat16 [768, 768], P('dp', 'tensor'), may hold values from -0.21875 to 0.21875
- w_value: bfloat16 [768, 768], P('dp', 'tensor'), may hold values from -0.21875 to 0.21875
- w_out: bfloat16 [768, 768], P('tensor', 'dp'), may hold values from -1.25 to 1.25
- b_query: bfloat16 [12, 64], P('tensor', 'dp'), may hold values from -3 to 3
- b_value: bfloat16 [12, 64], P('tensor', 'dp'), may hold values from -3 to 3
- w_up: bfloat16 [768, 3072], P('dp', 'tensor'), may hold values from -0.21875 to 0.21875
- w_down: bfloat16 [3072, 768], P('tensor', 'dp'), may hold values from -0.109375 to 0.109375
- b_up: bfloat16 [48, 64], P('tensor', 'dp'), may hold values from -3 to 3
- b_out: bfloat16 [768], P(('dp', 'tensor')), may hold values from -3 to 3
- gain_one: bfloat16 [768], P(('dp', 'tensor')), may hold values from 0.25 to 1.75
- shift_one: bfloat16 [768], P(('dp', 'tensor')), may hold values from -3 to 3
- b_down: bfloat16 [768], P(('dp', 'tensor')), may hold values from -3 to 3
- gain_two: bfloat16 [768], P(('dp', 'tensor')), may hold values from 0.25 to 1.75
- shift_two: bfloat16 [768], P(('dp', 'tensor')), may hold values from -3 to 3
- cotangent: float32 [16, 2048, 768], P('dp', 'tensor'), may hold values from -6 to 6
Outputs:
- layer_out: float32 [16, 2048, 768], P('dp', 'tensor')
- grad_tokens: float32 [16, 2048, 768], P('dp', 'tensor')
- grad_w_query: float32 [768, 768], P('dp', 'tensor')
- grad_w_key: float32 [768, 768], P('dp', 'tensor')
- grad_w_value: float32 [768, 768], P('dp', 'tensor')
- grad_w_out: float32 [768, 768], P('tensor', 'dp')
- grad_b_query: float32 [12, 64], P('tensor', 'dp')
- grad_b_value: float32 [12, 64], P('tensor', 'dp')
- grad_w_up: float32 [768, 3072], P('dp', 'tensor')
- grad_w_down: float32 [3072, 768], P('tensor', 'dp')
- grad_b_up: float32 [48, 64], P('tensor', 'dp')
- grad_b_out: float32 [768], P(('dp', 'tensor'))
- grad_gain_one: float32 [768], P(('dp', 'tensor'))
- grad_shift_one: float32 [768], P(('dp', 'tensor'))
- grad_b_down: float32 [768], P(('dp', 'tensor'))
- grad_gain_two: float32 [768], P(('dp', 'tensor'))
- grad_shift_two: float32 [768], P(('dp', 'tensor'))
The draws below stay inside these ranges and needn't reach their ends.
Inputs may be any that keep to these rules, and one draw needn't show every extreme that they name: `segment_ids`: in each sequence the segment numbers never fall and each of the 12 segments spans 1 to 1024 positions; some segment spans exactly 1024.
All inputs are finite; a program needn't handle non-finite values.
Results may differ from the reference program's by a relative error of at most 0.015.
Values may be sent and summed in bfloat16 or wider, within the bound.
No kernel may reach another device: no remote copies, remote signals or barrier semaphores. Data moves between devices by JAX's collectives and lax.ppermute only.
A program may use at most 192 MiB of HBM per device.

```python
import math
from functools import partial
import jax
import jax.numpy as jnp
import numpy as np
from jax import lax

HEADS = 12
HD = 64
FF = 3072
LEN = 2048
SEGS = 12
D = 768
SEQS = 16


def levels(own_key, extent, split, least, top_value):
    def one(dim, blocks):
        steps = jax.random.uniform(jax.random.fold_in(jax.random.fold_in(own_key, 6), dim), (blocks,), jnp.float32, least / len(split), top_value / len(split))
        return jnp.repeat(jnp.exp(steps), extent[dim] // blocks).reshape((-1,) + (1,) * (len(extent) - dim - 1))

    level = one(*split[0])
    for cut in split[1:]:
        level = level * one(*cut)
    return level


def profile(amount, total, limit, slope):
    loads = [(1 << 20) // math.isqrt(grade ** slope) + 1 for grade in range(2, amount + 1)]
    spare, counts = total - limit - (amount - 1), [1] * (amount - 1)
    while spare > 0:
        free = [i for i in range(amount - 1) if counts[i] < limit]
        whole, remaining = sum([loads[i] for i in free]), spare
        for i in free:
            more = min(limit - counts[i], max(1, remaining * loads[i] // whole), spare)
            counts[i] = counts[i] + more
            spare = spare - more
    return np.array([limit] + counts)


def uneven(stream_key, number_of, total, limit, lean):
    if number_of == 2:
        one = jax.random.randint(stream_key, (), max(1, total - limit), min(limit, total - 1) + 1)
        return jnp.stack([one, total - one])
    sizes = jnp.asarray(profile(number_of, total, limit, lean), jnp.int32)
    twos = (number_of - 1) // 2
    source_of, receiver = sizes[1:1 + 2 * twos:2], sizes[2:2 + 2 * twos:2]
    room = jnp.minimum(source_of - 1, limit - receiver)
    moved = jax.random.randint(jax.random.fold_in(stream_key, 1), (twos,), 0, 1 << 20) % (room + 1)
    sizes = sizes.at[1:1 + 2 * twos:2].set(source_of - moved).at[2:2 + 2 * twos:2].set(receiver + moved)
    return sizes[jax.random.permutation(jax.random.fold_in(stream_key, 2), number_of)]


def scatter_about(own_key, dims, deviation, bound, shards=(), held_as=jnp.bfloat16):
    drawn = jax.random.normal(own_key, dims, jnp.float32) * deviation
    if len(shards) > 0:
        drawn = levels(own_key, dims, shards, -0.22, 0.18) * drawn
    return jnp.clip(drawn, min=-bound, max=bound).astype(held_as)


def setup_inputs(seed: int = 0) -> dict:
    key_list = jax.random.split(jax.random.key(seed), 19)
    return {
        "tokens": scatter_about(key_list[0], (SEQS, LEN, D), 1.0, 6.0, ((0, 8), (1, 4))),
        "segment_ids": jax.vmap(lambda own: jnp.searchsorted(jnp.cumsum(uneven(own, SEGS, LEN, LEN // 2, 2)), jnp.arange(LEN), side="right"))(jax.random.split(key_list[1], SEQS)).reshape((SEQS, LEN)).astype(jnp.int32),
        "w_query": scatter_about(key_list[2], (D, D), D ** -0.5, 0.21875, ((0, 8), (1, 4))),
        "w_key": scatter_about(key_list[3], (D, D), D ** -0.5, 0.21875, ((0, 8), (1, 4))),
        "w_value": scatter_about(key_list[4], (D, D), D ** -0.5, 0.21875, ((0, 8), (1, 4))),
        "w_out": scatter_about(key_list[5], (D, D), (D // 32) ** -0.5, 1.25, ((0, 4), (1, 8))),
        "b_query": scatter_about(key_list[6], (HEADS, HD), 0.5, 3.0, ((0, 4), (1, 8))),
        "b_value": scatter_about(key_list[7], (HEADS, HD), 0.5, 3.0, ((0, 4), (1, 8))),
        "w_up": scatter_about(key_list[8], (D, FF), D ** -0.5, 0.21875, ((0, 8), (1, 4))),
        "w_down": scatter_about(key_list[9], (FF, D), FF ** -0.5, 0.109375, ((0, 4), (1, 8))),
        "b_up": scatter_about(key_list[10], (FF // HD, HD), 0.5, 3.0, ((0, 4), (1, 8))),
        "b_out": scatter_about(key_list[11], (D,), 0.5, 3.0, ((0, 32),)),
        "gain_one": jnp.clip(1.0 + 0.15 * jax.random.normal(key_list[12], (D,), jnp.float32), 0.25, 1.75).astype(jnp.bfloat16),
        "shift_one": scatter_about(key_list[13], (D,), 0.5, 3.0, ((0, 32),)),
        "b_down": scatter_about(key_list[14], (D,), 0.5, 3.0, ((0, 32),)),
        "gain_two": jnp.clip(1.0 + 0.15 * jax.random.normal(key_list[15], (D,), jnp.float32), 0.25, 1.75).astype(jnp.bfloat16),
        "shift_two": scatter_about(key_list[16], (D,), 0.5, 3.0, ((0, 32),)),
        "cotangent": scatter_about(key_list[17], (SEQS, LEN, D), 1.0, 6.0, ((0, 8), (1, 4)), jnp.float32),
    }


highest = lax.Precision.HIGHEST

@jax.custom_vjp
def low(v):
    return lax.optimization_barrier(v.astype(jnp.bfloat16)).astype(jnp.float32)

@jax.custom_vjp
def low_back(v):
    return v

def low_keep(v):
    return (low(v), None)

def low_pass(kept, grad):
    return (grad,)

def back_keep(v):
    return (v, None)

def back_low(kept, grad):
    return (low(grad),)
low.defvjp(low_keep, low_pass)
low_back.defvjp(back_keep, back_low)

def normalize(summed, gain, shift):
    centre = lax.optimization_barrier(jnp.mean(summed, axis=-1, keepdims=True))
    centred = summed - centre
    spread = lax.optimization_barrier(jnp.mean(centred * centred, axis=-1, keepdims=True))
    return centred * lax.rsqrt(spread + 1e-12) * gain + shift

def attend_sequence(members):
    queries, key_heads, value_heads, segments = members
    scores = jnp.einsum('qhd,khd->hqk', queries, key_heads, precision=highest) * HD ** (-0.5)
    scores = low_back(scores)
    same_doc = segments[:, None] == segments[None, :]
    scores = jnp.where(same_doc[None, :, :], scores, -1e+30)
    attention = low(jax.nn.softmax(scores, axis=-1))
    return jnp.einsum('hqk,khd->qhd', attention, value_heads, precision=highest)

def layer(segment_ids, tokens, w_query, w_key, w_value, w_out, b_query, b_value, w_up, w_down, b_up, b_out, gain_one, shift_one, b_down, gain_two, shift_two):
    sequences, length, features = tokens.shape
    flattened = tokens.reshape(sequences * length, features)

    def heads_of(product):
        return low_back(low(product)).reshape(sequences, length, HEADS, HD)
    queries = heads_of(jnp.dot(flattened, w_query, precision=highest) + b_query.reshape(features))
    key_heads = heads_of(jnp.dot(flattened, w_key, precision=highest))
    value_heads = heads_of(jnp.dot(flattened, w_value, precision=highest) + b_value.reshape(features))
    context = lax.map(jax.checkpoint(attend_sequence), (queries, key_heads, value_heads, segment_ids))
    context = low_back(low(context.reshape(sequences * length, features)))
    attended = low_back(jnp.dot(context, w_out, precision=highest))
    summed = flattened + attended + b_out
    normed = normalize(summed, gain_one, shift_one)
    hidden_input = low_back(jnp.dot(low(normed), w_up, precision=highest) + b_up.reshape(-1))
    activated = low(jax.nn.gelu(hidden_input, approximate=False))
    branch = low_back(jnp.dot(activated, w_down, precision=highest))
    result = normalize(normed + branch + b_down, gain_two, shift_two)
    return result.reshape(sequences, length, features)

def reference(tokens, segment_ids, w_query, w_key, w_value, w_out, b_query, b_value, w_up, w_down, b_up, b_out, gain_one, shift_one, b_down, gain_two, shift_two, cotangent):
    inputs = [array.astype(jnp.float32) for array in (tokens, w_query, w_key, w_value, w_out, b_query, b_value, w_up, w_down, b_up, b_out, gain_one, shift_one, b_down, gain_two, shift_two)]
    result, pullback = jax.vjp(partial(layer, segment_ids), *inputs)
    grads = pullback(cotangent.astype(jnp.float32))
    return (result, grads[0], grads[1], grads[2], grads[3], grads[4], grads[5], grads[6], grads[7], grads[8], grads[9], grads[10], grads[11], grads[12], grads[13], grads[14], grads[15])
```

```python
import jax
import jax.numpy as jnp
from jax import lax
from jax.experimental import pallas as pl
from jax.experimental.pallas import tpu as pltpu
from jax.sharding import PartitionSpec as P

HD = 64
PAIR = 2 * HD
SEGS = 12
QB = 256
KB = 256
NEG = -1e30
EPS = 1e-12
BF = jnp.bfloat16
F32 = jnp.float32
BOTH = ("dp", "tensor")
NT = (((1,), (1,)), ((), ()))


def head_parts(block, scale=None):
    wide = block.astype(F32)
    if scale is not None:
        wide = wide * scale
    lane = lax.broadcasted_iota(jnp.int32, block.shape, 1)
    first = jnp.where(lane < HD, wide, 0.0).astype(BF)
    second = jnp.where(lane >= HD, wide, 0.0).astype(BF)
    return first, second


def attention_forward_kernel(lo_ref, hi_ref, bound_ref, q_ref, k_ref, v_ref, o_ref, lse_ref, vt_ref, acc_ref):
    row = pl.program_id(1)

    @pl.when(row == 0)
    def _():
        vt_ref[...] = v_ref[...].T

    parts = head_parts(q_ref[...], HD ** (-0.5))
    start = bound_ref[0, 0:1, :]
    end = bound_ref[0, 1:2, :]
    acc_ref[...] = jnp.zeros_like(acc_ref)

    def step(kb, carry):
        base = pl.multiple_of(kb * KB, KB)
        keys = k_ref[pl.ds(base, KB), :]
        place = base + lax.broadcasted_iota(jnp.int32, (KB, QB), 0)
        valid = (place >= start) & (place < end)
        after = []
        for h in range(2):
            top, total = carry[2 * h], carry[2 * h + 1]
            scores = lax.dot_general(keys, parts[h], NT, preferred_element_type=F32)
            scores = jnp.where(valid, scores, NEG)
            new_top = jnp.maximum(top, jnp.max(scores, axis=0, keepdims=True))
            fade = jnp.exp(top - new_top)
            raised = jnp.exp(scores - new_top)
            total = fade * total + jnp.sum(raised, axis=0, keepdims=True)
            rows = slice(h * HD, (h + 1) * HD)
            acc_ref[rows, :] = fade * acc_ref[rows, :] + jnp.dot(
                vt_ref[rows, pl.ds(base, KB)], raised.astype(BF), preferred_element_type=F32
            )
            after += [new_top, total]
        return tuple(after)

    low = jnp.full((1, QB), NEG, F32)
    none = jnp.zeros((1, QB), F32)
    top0, total0, top1, total1 = lax.fori_loop(lo_ref[row], hi_ref[row], step, (low, none, low, none))
    acc_ref[0:HD, :] = acc_ref[0:HD, :] / total0
    acc_ref[HD:PAIR, :] = acc_ref[HD:PAIR, :] / total1
    o_ref[...] = acc_ref[...].T.astype(BF)
    lse_ref[0, 0, 0:1, :] = top0 + jnp.log(total0)
    lse_ref[0, 0, 1:2, :] = top1 + jnp.log(total1)


def attention_backward_kernel(
    lo_ref, hi_ref, bound_ref, lse_ref, q_ref, k_ref, v_ref, do_ref, o_ref, out_ref, kt_ref, dq_ref, dk_ref, dv_ref
):
    row = pl.program_id(1)

    @pl.when(row == 0)
    def _():
        kt_ref[...] = k_ref[...].T
        dk_ref[...] = jnp.zeros_like(dk_ref)
        dv_ref[...] = jnp.zeros_like(dv_ref)

    q_parts = head_parts(q_ref[...], HD ** (-0.5))
    grad = do_ref[...]
    g_parts = head_parts(grad)
    start = bound_ref[0, 0:1, :]
    end = bound_ref[0, 1:2, :]
    product = grad.astype(F32) * o_ref[...].astype(F32)
    picker_row = lax.broadcasted_iota(jnp.int32, (8, PAIR), 0)
    picker_lane = lax.broadcasted_iota(jnp.int32, (8, PAIR), 1)
    picker = jnp.where(picker_lane // HD == picker_row, 1.0, 0.0).astype(F32)
    inner = lax.dot_general(picker, product, NT, precision=lax.Precision.HIGHEST, preferred_element_type=F32)
    dq_ref[...] = jnp.zeros_like(dq_ref)

    def step(kb, carry):
        base = pl.multiple_of(kb * KB, KB)
        keys = k_ref[pl.ds(base, KB), :]
        vals = v_ref[pl.ds(base, KB), :]
        place = base + lax.broadcasted_iota(jnp.int32, (KB, QB), 0)
        valid = (place >= start) & (place < end)
        dk = dk_ref[pl.ds(base, KB), :]
        dv = dv_ref[pl.ds(base, KB), :]
        for h in range(2):
            scores = lax.dot_general(keys, q_parts[h], NT, preferred_element_type=F32)
            scores = jnp.where(valid, scores, NEG)
            weights = jnp.exp(scores - lse_ref[0, 0, h : h + 1, :])
            grad_weights = lax.dot_general(vals, g_parts[h], NT, preferred_element_type=F32)
            grad_scores = (weights * (grad_weights - inner[h : h + 1, :])).astype(BF)
            dv = dv + jnp.dot(weights.astype(BF), g_parts[h], preferred_element_type=F32)
            dk = dk + jnp.dot(grad_scores, q_parts[h], preferred_element_type=F32)
            rows = slice(h * HD, (h + 1) * HD)
            dq_ref[rows, :] += jnp.dot(kt_ref[rows, pl.ds(base, KB)], grad_scores, preferred_element_type=F32)
        dk_ref[pl.ds(base, KB), :] = dk
        dv_ref[pl.ds(base, KB), :] = dv
        return carry

    lax.fori_loop(lo_ref[row], hi_ref[row], step, 0)
    out_ref[pl.ds(pl.multiple_of(row * QB, QB), QB), 0:PAIR] = (dq_ref[...] * HD ** (-0.5)).T.astype(BF)

    @pl.when(row == pl.num_programs(1) - 1)
    def _():
        out_ref[:, PAIR : 2 * PAIR] = dk_ref[...].astype(BF)
        out_ref[:, 2 * PAIR : 3 * PAIR] = dv_ref[...].astype(BF)


def attention_forward(qkv, lo, hi, bounds):
    length = qkv.shape[0]
    pairs = qkv.shape[1] // (3 * PAIR)
    blocks = length // QB
    return pl.pallas_call(
        attention_forward_kernel,
        name="attention_forward",
        out_shape=(
            jax.ShapeDtypeStruct((length, pairs * PAIR), BF),
            jax.ShapeDtypeStruct((pairs, blocks, 2, QB), F32),
        ),
        grid_spec=pltpu.PrefetchScalarGridSpec(
            num_scalar_prefetch=2,
            grid=(pairs, blocks),
            in_specs=[
                pl.BlockSpec((1, 2, QB), lambda j, i, lo, hi: (i, 0, 0)),
                pl.BlockSpec((QB, PAIR), lambda j, i, lo, hi: (i, 3 * j)),
                pl.BlockSpec((length, PAIR), lambda j, i, lo, hi: (0, 3 * j + 1)),
                pl.BlockSpec((length, PAIR), lambda j, i, lo, hi: (0, 3 * j + 2)),
            ],
            out_specs=(
                pl.BlockSpec((QB, PAIR), lambda j, i, lo, hi: (i, j)),
                pl.BlockSpec((1, 1, 2, QB), lambda j, i, lo, hi: (j, i, 0, 0)),
            ),
            scratch_shapes=[pltpu.VMEM((PAIR, length), BF), pltpu.VMEM((PAIR, QB), F32)],
        ),
        cost_estimate=pl.CostEstimate(
            flops=pairs * length * length * PAIR * 4,
            transcendentals=pairs * length * length,
            bytes_accessed=qkv.size * 2 + length * pairs * PAIR * 2,
        ),
        compiler_params=pltpu.CompilerParams(dimension_semantics=("arbitrary", "arbitrary")),
    )(lo, hi, bounds, qkv, qkv, qkv)


def attention_backward(qkv, grad, out, lse, lo, hi, bounds):
    length = qkv.shape[0]
    pairs = qkv.shape[1] // (3 * PAIR)
    blocks = length // QB
    return pl.pallas_call(
        attention_backward_kernel,
        name="attention_backward",
        out_shape=jax.ShapeDtypeStruct(qkv.shape, BF),
        grid_spec=pltpu.PrefetchScalarGridSpec(
            num_scalar_prefetch=2,
            grid=(pairs, blocks),
            in_specs=[
                pl.BlockSpec((1, 2, QB), lambda j, i, lo, hi: (i, 0, 0)),
                pl.BlockSpec((1, 1, 2, QB), lambda j, i, lo, hi: (j, i, 0, 0)),
                pl.BlockSpec((QB, PAIR), lambda j, i, lo, hi: (i, 3 * j)),
                pl.BlockSpec((length, PAIR), lambda j, i, lo, hi: (0, 3 * j + 1)),
                pl.BlockSpec((length, PAIR), lambda j, i, lo, hi: (0, 3 * j + 2)),
                pl.BlockSpec((QB, PAIR), lambda j, i, lo, hi: (i, j)),
                pl.BlockSpec((QB, PAIR), lambda j, i, lo, hi: (i, j)),
            ],
            out_specs=pl.BlockSpec((length, 3 * PAIR), lambda j, i, lo, hi: (0, j)),
            scratch_shapes=[
                pltpu.VMEM((PAIR, length), BF),
                pltpu.VMEM((PAIR, QB), F32),
                pltpu.VMEM((length, PAIR), F32),
                pltpu.VMEM((length, PAIR), F32),
            ],
        ),
        cost_estimate=pl.CostEstimate(
            flops=pairs * length * length * PAIR * 10,
            transcendentals=pairs * length * length,
            bytes_accessed=qkv.size * 4 + length * pairs * PAIR * 4,
        ),
        compiler_params=pltpu.CompilerParams(dimension_semantics=("arbitrary", "arbitrary")),
    )(lo, hi, bounds, lse, qkv, qkv, qkv, grad, out)


def segment_bounds(segments):
    length = segments.shape[0]
    names = jnp.arange(SEGS, dtype=jnp.int32)[:, None]
    counts = jnp.sum((segments[None, :] == names).astype(jnp.int32), axis=1, keepdims=True)
    start = jnp.sum(jnp.where(segments[None, :] > names, counts, 0), axis=0)
    end = jnp.sum(jnp.where(segments[None, :] >= names, counts, 0), axis=0)
    start = start.reshape(length // QB, QB)
    end = end.reshape(length // QB, QB)
    lo = start[:, 0] // KB
    hi = (end[:, -1] + (KB - 1)) // KB
    return lo, hi, jnp.stack([start, end], axis=1)


def statistics(rows):
    centred = rows - jnp.mean(rows, axis=-1, keepdims=True)
    inverse = lax.rsqrt(jnp.mean(centred * centred, axis=-1, keepdims=True) + EPS)
    return centred * inverse, inverse


def norm_backward(grad, hat, inverse, gain):
    scaled = grad * gain
    return inverse * (
        scaled
        - jnp.mean(scaled, axis=-1, keepdims=True)
        - hat * jnp.mean(scaled * hat, axis=-1, keepdims=True)
    )


def mm(a, b):
    return lax.dot_general(a, b, (((1,), (0,)), ((), ())), preferred_element_type=F32)


def mm_nt(a, b):
    return lax.dot_general(a, b, NT, preferred_element_type=F32)


def mm_tn(a, b):
    return lax.dot_general(a, b, (((0,), (0,)), ((), ())), preferred_element_type=F32)


def make_per_device(dp):
    def per_device(
        tokens,
        segment_ids,
        w_query,
        w_key,
        w_value,
        w_out,
        b_query,
        b_value,
        w_up,
        w_down,
        b_up,
        b_out,
        gain_one,
        shift_one,
        b_down,
        gain_two,
        shift_two,
        cotangent,
    ):
        place = lax.axis_index("tensor")
        across = place // 2
        core = place % 2
        _, quarter, features = tokens.shape
        cut, columns = w_query.shape
        units = w_up.shape[1]
        half = 2 * columns
        first_core = core == 0
        first_chip = across == 0

        def swap_chips(value):
            return lax.ppermute(value, "tensor", [(0, 2), (2, 0), (1, 3), (3, 1)])

        def swap_cores(value):
            return lax.ppermute(value, "tensor", [(0, 1), (1, 0), (2, 3), (3, 2)])

        def in_order(flag, mine, other, axis):
            return jnp.stack([jnp.where(flag, mine, other), jnp.where(flag, other, mine)], axis=axis)

        def mine_of(value, index, axis):
            return lax.dynamic_index_in_dim(value, index, axis, keepdims=False)

        tokens_own = in_order(first_chip, mine_of(tokens, across, 0), swap_chips(mine_of(tokens, 1 - across, 0)), 0)
        tokens_low = tokens_own
        tokens_full = in_order(first_core, tokens_low, swap_cores(tokens_low), 1).reshape(4 * quarter, features)
        tokens_own = tokens_own.reshape(2 * quarter, features)
        cotangent_own = in_order(
            first_chip,
            mine_of(cotangent, across, 0),
            swap_chips(mine_of(cotangent, 1 - across, 0).astype(BF)).astype(F32),
            0,
        ).reshape(2 * quarter, features)
        segments = mine_of(segment_ids, across, 0)
        lo, hi, bounds = segment_bounds(segments)

        small = [b_query, b_value, b_up, b_out, gain_one, shift_one, b_down, gain_two, shift_two]
        sizes = [v.size for v in small]
        small_rows = -(-sum(sizes) // features)
        packed = jnp.concatenate([v.reshape(-1) for v in small])
        packed = jnp.pad(packed, (0, small_rows * features - packed.size)).reshape(small_rows, features)
        first_pack = jnp.concatenate([jnp.concatenate([w_query, w_key, w_value, w_out.T], axis=1), packed], axis=0)
        first_all = lax.all_gather(first_pack, BOTH, axis=0).reshape(dp, 4, cut + small_rows, features)
        second_pack = jnp.stack([w_up, w_down.T], axis=0)
        second_all = lax.all_gather(second_pack, BOTH, axis=0).reshape(dp, 4, 2, cut, units)

        attention_all = first_all[:, :, :cut, :]
        qkv_mine = mine_of(attention_all[..., : 3 * columns].reshape(dp, 2, 2, cut, 3, columns), core, 2)
        pairs = half // PAIR
        w_qkv = (
            qkv_mine.transpose(0, 2, 3, 1, 4)
            .reshape(features, 3, pairs, PAIR)
            .transpose(0, 2, 1, 3)
            .reshape(features, 3 * half)
        )
        w_out_t = (
            attention_all[..., 3 * columns :]
            .reshape(dp, 2, 2, cut, columns)
            .transpose(0, 3, 2, 1, 4)
            .reshape(features, features)
        )
        small_all = first_all[:, :, cut:, :].reshape(dp, 4, small_rows * features)
        pieces = []
        offset = 0
        for v, size in zip(small, sizes):
            piece = small_all[:, :, offset : offset + size]
            offset += size
            if v.ndim == 2:
                piece = piece.reshape(dp, 4, *v.shape).transpose(1, 2, 0, 3)
                pieces.append(piece.reshape(4 * v.shape[0], dp * v.shape[1]).astype(F32))
            else:
                pieces.append(piece.reshape(-1).astype(F32))
        bias_q, bias_v, bias_up, out_bias, gain1, shift1, down_bias, gain2, shift2 = pieces
        w_up_full = second_all[:, :, 0].transpose(0, 2, 1, 3).reshape(features, 4 * units)
        w_down_t = second_all[:, :, 1].transpose(0, 2, 1, 3).reshape(features, 4 * units)

        def my_bias(bias):
            return mine_of(bias.reshape(2, 2, columns), core, 1).reshape(pairs, PAIR)

        bias_mine = jnp.stack([my_bias(bias_q), jnp.zeros((pairs, PAIR), F32), my_bias(bias_v)], axis=1)
        qkv = (mm(tokens_full, w_qkv) + bias_mine.reshape(-1)).astype(BF)
        heads_out, lse = attention_forward(qkv, lo, hi, bounds)

        by_core = heads_out.reshape(2, 2, quarter, half)
        kept = mine_of(by_core, core, 1)
        got = swap_cores(mine_of(by_core, 1 - core, 1))
        context = in_order(first_core, kept, got, 2).reshape(2 * quarter, 2 * half)

        summed = tokens_own.astype(F32) + mm_nt(context, w_out_t) + out_bias
        hat1, inverse1 = statistics(summed)
        normed = hat1 * gain1 + shift1
        normed_low = normed.astype(BF)
        hidden = mm(normed_low, w_up_full) + bias_up.reshape(-1)
        area = 0.5 * (1.0 + lax.erf(hidden * (2.0 ** -0.5)))
        activated = (hidden * area).astype(BF)
        slope = (area + hidden * jnp.exp(-0.5 * hidden * hidden) * ((2.0 * jnp.pi) ** -0.5)).astype(BF)
        hat2, inverse2 = statistics(normed + mm_nt(activated, w_down_t) + down_bias)
        out_own = (hat2 * gain2 + shift2).reshape(2, quarter, features)

        def send_back(value):
            kept_part = mine_of(value, across, 0)
            got_part = swap_chips(mine_of(value, 1 - across, 0).astype(BF)).astype(F32)
            return in_order(first_chip, kept_part, got_part, 0)

        layer_out = send_back(out_own)

        grad_z = norm_backward(cotangent_own, hat2, inverse2, gain2)
        grad_branch = grad_z.astype(BF)
        grad_down_t = mm_tn(grad_branch, activated)
        grad_hidden = (mm(grad_branch, w_down_t) * slope.astype(F32)).astype(BF)
        grad_up = mm_tn(normed_low, grad_hidden)
        grad_normed = grad_z + mm_nt(grad_hidden, w_up_full)
        grad_summed = norm_backward(grad_normed, hat1, inverse1, gain1)
        grad_attended = grad_summed.astype(BF)
        grad_out_t = mm_tn(grad_attended, context)
        grad_context = mm(grad_attended, w_out_t).astype(BF).reshape(2, quarter, 2, half)
        kept = mine_of(grad_context, core, 2)
        got = swap_cores(mine_of(grad_context, 1 - core, 2))
        grad_heads = in_order(first_core, kept, got, 1).reshape(4 * quarter, half)

        def to_blocks(grad):
            return grad.astype(BF).reshape(dp, cut, 4, units).transpose(0, 2, 1, 3)

        second_grads = jnp.stack([to_blocks(grad_up), to_blocks(grad_down_t)], axis=2).reshape(4 * dp, 2 * cut, units)
        second_mine = lax.psum_scatter(second_grads, BOTH, scatter_dimension=0, tiled=False)

        grad_qkv = attention_backward(qkv, grad_heads, heads_out, lse, lo, hi, bounds)
        grad_w_qkv = (
            mm_tn(tokens_full, grad_qkv)
            .astype(BF)
            .reshape(dp, cut, pairs, 3, PAIR)
            .transpose(0, 1, 3, 2, 4)
            .reshape(dp, cut, 3, 2, columns)
            .transpose(0, 3, 1, 2, 4)
            .reshape(dp, 2, cut, 3 * columns)
        )
        bias_grads = jnp.sum(grad_qkv.astype(F32), axis=0).reshape(pairs, 3, PAIR)
        part = mm_nt(grad_qkv, w_qkv).reshape(2, 2, quarter, features)
        part_kept = mine_of(part, core, 1)
        part_got = swap_cores(mine_of(part, 1 - core, 1).astype(BF))
        grad_tokens = send_back(
            grad_summed.reshape(2, quarter, features) + part_kept + part_got.astype(F32)
        )

        def for_both_cores(value, axis):
            zero = jnp.zeros_like(value)
            return jnp.stack(
                [jnp.where(first_core, value, zero), jnp.where(first_core, zero, value)], axis=axis
            )

        qkv_blocks = for_both_cores(grad_w_qkv, 2).reshape(dp, 4, cut, 3 * columns)
        out_blocks = (
            grad_out_t.astype(BF)
            .reshape(dp, cut, 2, 2, columns)
            .transpose(0, 3, 2, 1, 4)
            .reshape(dp, 4, cut, columns)
        )

        def matrix_small(value, like):
            return value.reshape(4, like.shape[0], dp, like.shape[1]).transpose(2, 0, 1, 3).reshape(dp, 4, -1)

        def head_small(value, like):
            return matrix_small(for_both_cores(value.reshape(2, columns), 1), like)

        def vector_small(value):
            return value.reshape(dp, 4, -1)

        small_grads = jnp.concatenate(
            [
                head_small(bias_grads[:, 0], b_query),
                head_small(bias_grads[:, 2], b_value),
                matrix_small(jnp.sum(grad_hidden.astype(F32), axis=0), b_up),
                vector_small(jnp.sum(grad_summed, axis=0)),
                vector_small(jnp.sum(grad_normed * hat1, axis=0)),
                vector_small(jnp.sum(grad_normed, axis=0)),
                vector_small(jnp.sum(grad_z, axis=0)),
                vector_small(jnp.sum(cotangent_own * hat2, axis=0)),
                vector_small(jnp.sum(cotangent_own, axis=0)),
            ],
            axis=2,
        ).astype(BF)
        small_grads = jnp.pad(small_grads, ((0, 0), (0, 0), (0, small_rows * features - small_grads.shape[2])))
        first_grads = jnp.concatenate(
            [
                jnp.concatenate([qkv_blocks, out_blocks], axis=3),
                small_grads.reshape(dp, 4, small_rows, features),
            ],
            axis=2,
        ).reshape(4 * dp, cut + small_rows, features)
        first_mine = lax.psum_scatter(first_grads, BOTH, scatter_dimension=0, tiled=False).astype(F32)
        second_mine = second_mine.astype(F32)

        attention_mine = first_mine[:cut]
        small_mine = first_mine[cut:].reshape(-1)
        small_out = []
        offset = 0
        for v, size in zip(small, sizes):
            small_out.append(small_mine[offset : offset + size].reshape(v.shape))
            offset += size
        return (
            layer_out,
            grad_tokens,
            attention_mine[:, :columns],
            attention_mine[:, columns : 2 * columns],
            attention_mine[:, 2 * columns : 3 * columns],
            attention_mine[:, 3 * columns :].T,
            small_out[0],
            small_out[1],
            second_mine[:cut],
            second_mine[cut:].T,
            small_out[2],
            small_out[3],
            small_out[4],
            small_out[5],
            small_out[6],
            small_out[7],
            small_out[8],
        )

    return per_device


def solution(mesh):
    rows = P("dp", "tensor", None)
    split = P("dp", "tensor")
    turned = P("tensor", "dp")
    vector = P(("dp", "tensor"))
    in_specs = (rows, P("dp", None), split, split, split, turned, turned, turned, split, turned, turned)
    in_specs += (vector,) * 6 + (rows,)
    out_specs = (rows, rows, split, split, split, turned, turned, turned, split, turned, turned)
    out_specs += (vector,) * 6
    return jax.shard_map(
        make_per_device(mesh.shape["dp"]), mesh=mesh, in_specs=in_specs, out_specs=out_specs, check_vma=False
    )
```

```python
import jax
import jax.numpy as jnp
from jax import lax
from jax.experimental import pallas as pl
from jax.experimental.pallas import tpu as pltpu
from jax.sharding import PartitionSpec as P

HD = 64
PAIR = 2 * HD
SEGS = 12
QB = 256
KB = 256
NEG = -1e30
EPS = 1e-12
BF = jnp.bfloat16
F32 = jnp.float32
BOTH = ("dp", "tensor")
NT = (((1,), (1,)), ((), ()))


def head_parts(block, scale=None):
    wide = block.astype(F32)
    if scale is not None:
        wide = wide * scale
    lane = lax.broadcasted_iota(jnp.int32, block.shape, 1)
    first = jnp.where(lane < HD, wide, 0.0).astype(BF)
    second = jnp.where(lane >= HD, wide, 0.0).astype(BF)
    return first, second


def attention_forward_kernel(lo_ref, hi_ref, bound_ref, q_ref, k_ref, v_ref, o_ref, lse_ref, vt_ref, acc_ref):
    row = pl.program_id(1)

    @pl.when(row == 0)
    def _():
        vt_ref[...] = v_ref[...].T

    parts = head_parts(q_ref[...], HD ** (-0.5))
    start = bound_ref[0, 0:1, :]
    end = bound_ref[0, 1:2, :]
    acc_ref[...] = jnp.zeros_like(acc_ref)

    def step(kb, carry):
        base = pl.multiple_of(kb * KB, KB)
        keys = k_ref[pl.ds(base, KB), :]
        place = base + lax.broadcasted_iota(jnp.int32, (KB, QB), 0)
        valid = (place >= start) & (place < end)
        after = []
        for h in range(2):
            top, total = carry[2 * h], carry[2 * h + 1]
            scores = lax.dot_general(keys, parts[h], NT, preferred_element_type=F32)
            scores = jnp.where(valid, scores, NEG)
            new_top = jnp.maximum(top, jnp.max(scores, axis=0, keepdims=True))
            fade = jnp.exp(top - new_top)
            raised = jnp.exp(scores - new_top)
            total = fade * total + jnp.sum(raised, axis=0, keepdims=True)
            rows = slice(h * HD, (h + 1) * HD)
            acc_ref[rows, :] = fade * acc_ref[rows, :] + jnp.dot(
                vt_ref[rows, pl.ds(base, KB)], raised.astype(BF), preferred_element_type=F32
            )
            after += [new_top, total]
        return tuple(after)

    low = jnp.full((1, QB), NEG, F32)
    none = jnp.zeros((1, QB), F32)
    top0, total0, top1, total1 = lax.fori_loop(lo_ref[row], hi_ref[row], step, (low, none, low, none))
    acc_ref[0:HD, :] = acc_ref[0:HD, :] / total0
    acc_ref[HD:PAIR, :] = acc_ref[HD:PAIR, :] / total1
    o_ref[...] = acc_ref[...].T.astype(BF)
    lse_ref[0, 0, 0:1, :] = top0 + jnp.log(total0)
    lse_ref[0, 0, 1:2, :] = top1 + jnp.log(total1)


def attention_backward_kernel(
    lo_ref, hi_ref, bound_ref, lse_ref, q_ref, k_ref, v_ref, do_ref, o_ref, out_ref, kt_ref, dq_ref, dk_ref, dv_ref
):
    row = pl.program_id(1)

    @pl.when(row == 0)
    def _():
        kt_ref[...] = k_ref[...].T
        dk_ref[...] = jnp.zeros_like(dk_ref)
        dv_ref[...] = jnp.zeros_like(dv_ref)

    q_parts = head_parts(q_ref[...], HD ** (-0.5))
    grad = do_ref[...]
    g_parts = head_parts(grad)
    start = bound_ref[0, 0:1, :]
    end = bound_ref[0, 1:2, :]
    product = grad.astype(F32) * o_ref[...].astype(F32)
    picker_row = lax.broadcasted_iota(jnp.int32, (8, PAIR), 0)
    picker_lane = lax.broadcasted_iota(jnp.int32, (8, PAIR), 1)
    picker = jnp.where(picker_lane // HD == picker_row, 1.0, 0.0).astype(F32)
    inner = lax.dot_general(picker, product, NT, precision=lax.Precision.HIGHEST, preferred_element_type=F32)
    dq_ref[...] = jnp.zeros_like(dq_ref)

    def step(kb, carry):
        base = pl.multiple_of(kb * KB, KB)
        keys = k_ref[pl.ds(base, KB), :]
        vals = v_ref[pl.ds(base, KB), :]
        place = base + lax.broadcasted_iota(jnp.int32, (KB, QB), 0)
        valid = (place >= start) & (place < end)
        dk = dk_ref[pl.ds(base, KB), :]
        dv = dv_ref[pl.ds(base, KB), :]
        for h in range(2):
            scores = lax.dot_general(keys, q_parts[h], NT, preferred_element_type=F32)
            scores = jnp.where(valid, scores, NEG)
            weights = jnp.exp(scores - lse_ref[0, 0, h : h + 1, :])
            grad_weights = lax.dot_general(vals, g_parts[h], NT, preferred_element_type=F32)
            grad_scores = (weights * (grad_weights - inner[h : h + 1, :])).astype(BF)
            dv = dv + jnp.dot(weights.astype(BF), g_parts[h], preferred_element_type=F32)
            dk = dk + jnp.dot(grad_scores, q_parts[h], preferred_element_type=F32)
            rows = slice(h * HD, (h + 1) * HD)
            dq_ref[rows, :] += jnp.dot(kt_ref[rows, pl.ds(base, KB)], grad_scores, preferred_element_type=F32)
        dk_ref[pl.ds(base, KB), :] = dk
        dv_ref[pl.ds(base, KB), :] = dv
        return carry

    lax.fori_loop(lo_ref[row], hi_ref[row], step, 0)
    out_ref[pl.ds(pl.multiple_of(row * QB, QB), QB), 0:PAIR] = (dq_ref[...] * HD ** (-0.5)).T.astype(BF)

    @pl.when(row == pl.num_programs(1) - 1)
    def _():
        out_ref[:, PAIR : 2 * PAIR] = dk_ref[...].astype(BF)
        out_ref[:, 2 * PAIR : 3 * PAIR] = dv_ref[...].astype(BF)


def attention_forward(qkv, lo, hi, bounds):
    length = qkv.shape[0]
    pairs = qkv.shape[1] // (3 * PAIR)
    blocks = length // QB
    return pl.pallas_call(
        attention_forward_kernel,
        name="attention_forward",
        out_shape=(
            jax.ShapeDtypeStruct((length, pairs * PAIR), BF),
            jax.ShapeDtypeStruct((pairs, blocks, 2, QB), F32),
        ),
        grid_spec=pltpu.PrefetchScalarGridSpec(
            num_scalar_prefetch=2,
            grid=(pairs, blocks),
            in_specs=[
                pl.BlockSpec((1, 2, QB), lambda j, i, lo, hi: (i, 0, 0)),
                pl.BlockSpec((QB, PAIR), lambda j, i, lo, hi: (i, 3 * j)),
                pl.BlockSpec((length, PAIR), lambda j, i, lo, hi: (0, 3 * j + 1)),
                pl.BlockSpec((length, PAIR), lambda j, i, lo, hi: (0, 3 * j + 2)),
            ],
            out_specs=(
                pl.BlockSpec((QB, PAIR), lambda j, i, lo, hi: (i, j)),
                pl.BlockSpec((1, 1, 2, QB), lambda j, i, lo, hi: (j, i, 0, 0)),
            ),
            scratch_shapes=[pltpu.VMEM((PAIR, length), BF), pltpu.VMEM((PAIR, QB), F32)],
        ),
        cost_estimate=pl.CostEstimate(
            flops=pairs * length * length * PAIR * 4,
            transcendentals=pairs * length * length,
            bytes_accessed=qkv.size * 2 + length * pairs * PAIR * 2,
        ),
        compiler_params=pltpu.CompilerParams(dimension_semantics=("arbitrary", "arbitrary")),
    )(lo, hi, bounds, qkv, qkv, qkv)


def attention_backward(qkv, grad, out, lse, lo, hi, bounds):
    length = qkv.shape[0]
    pairs = qkv.shape[1] // (3 * PAIR)
    blocks = length // QB
    return pl.pallas_call(
        attention_backward_kernel,
        name="attention_backward",
        out_shape=jax.ShapeDtypeStruct(qkv.shape, BF),
        grid_spec=pltpu.PrefetchScalarGridSpec(
            num_scalar_prefetch=2,
            grid=(pairs, blocks),
            in_specs=[
                pl.BlockSpec((1, 2, QB), lambda j, i, lo, hi: (i, 0, 0)),
                pl.BlockSpec((1, 1, 2, QB), lambda j, i, lo, hi: (j, i, 0, 0)),
                pl.BlockSpec((QB, PAIR), lambda j, i, lo, hi: (i, 3 * j)),
                pl.BlockSpec((length, PAIR), lambda j, i, lo, hi: (0, 3 * j + 1)),
                pl.BlockSpec((length, PAIR), lambda j, i, lo, hi: (0, 3 * j + 2)),
                pl.BlockSpec((QB, PAIR), lambda j, i, lo, hi: (i, j)),
                pl.BlockSpec((QB, PAIR), lambda j, i, lo, hi: (i, j)),
            ],
            out_specs=pl.BlockSpec((length, 3 * PAIR), lambda j, i, lo, hi: (0, j)),
            scratch_shapes=[
                pltpu.VMEM((PAIR, length), BF),
                pltpu.VMEM((PAIR, QB), F32),
                pltpu.VMEM((length, PAIR), F32),
                pltpu.VMEM((length, PAIR), F32),
            ],
        ),
        cost_estimate=pl.CostEstimate(
            flops=pairs * length * length * PAIR * 10,
            transcendentals=pairs * length * length,
            bytes_accessed=qkv.size * 4 + length * pairs * PAIR * 4,
        ),
        compiler_params=pltpu.CompilerParams(dimension_semantics=("arbitrary", "arbitrary")),
    )(lo, hi, bounds, lse, qkv, qkv, qkv, grad, out)


def segment_bounds(segments):
    length = segments.shape[0]
    names = jnp.arange(SEGS, dtype=jnp.int32)[:, None]
    counts = jnp.sum((segments[None, :] == names).astype(jnp.int32), axis=1, keepdims=True)
    start = jnp.sum(jnp.where(segments[None, :] > names, counts, 0), axis=0)
    end = jnp.sum(jnp.where(segments[None, :] >= names, counts, 0), axis=0)
    start = start.reshape(length // QB, QB)
    end = end.reshape(length // QB, QB)
    lo = start[:, 0] // KB
    hi = (end[:, -1] + (KB - 1)) // KB
    return lo, hi, jnp.stack([start, end], axis=1)


def statistics(rows):
    centred = rows - jnp.mean(rows, axis=-1, keepdims=True)
    inverse = lax.rsqrt(jnp.mean(centred * centred, axis=-1, keepdims=True) + EPS)
    return centred * inverse, inverse


def norm_backward(grad, hat, inverse, gain):
    scaled = grad * gain
    return inverse * (
        scaled
        - jnp.mean(scaled, axis=-1, keepdims=True)
        - hat * jnp.mean(scaled * hat, axis=-1, keepdims=True)
    )


def mm(a, b):
    return lax.dot_general(a, b, (((1,), (0,)), ((), ())), preferred_element_type=F32)


def mm_nt(a, b):
    return lax.dot_general(a, b, NT, preferred_element_type=F32)


def mm_tn(a, b):
    return lax.dot_general(a, b, (((0,), (0,)), ((), ())), preferred_element_type=F32)


def piece_rows(ref):
    block = ref[:, 0]
    return block.reshape(block.shape[0] * block.shape[1], block.shape[2])


def project_kernel(spot_ref, tokens_ref, weights_ref, bias_ref, qkv_ref, w_ref):
    slots, cut, width = weights_ref.shape
    columns = width // 3
    bits = (slots // 2).bit_length() - 1

    @pl.when(pl.program_id(0) == 0)
    def _():
        for d in range(slots // 2):
            other = d ^ spot_ref[0]
            slot = 0
            for b in range(bits):
                slot = slot * 2 + ((other >> b) & 1)
            first = weights_ref[slot * 2 + spot_ref[1]].astype(F32)
            second = weights_ref[slot * 2 + 1 - spot_ref[1]].astype(F32)
            for s in range(3):
                cols = slice(s * columns, (s + 1) * columns)
                joined = jnp.concatenate([first[:, cols], second[:, cols]], axis=1).astype(BF)
                for p in range(2 * columns // PAIR):
                    at = (3 * p + s) * PAIR
                    w_ref[d * cut : (d + 1) * cut, at : at + PAIR] = joined[:, p * PAIR : (p + 1) * PAIR]

    qkv_ref[...] = (mm(tokens_ref[...], w_ref[...]) + bias_ref[...]).astype(BF)


def project(tokens, weights, bias, spot):
    length, features = tokens.shape
    width = 2 * weights.shape[2]
    return pl.pallas_call(
        project_kernel,
        name="project",
        out_shape=(
            jax.ShapeDtypeStruct((length, width), BF),
            jax.ShapeDtypeStruct((features, width), BF),
        ),
        grid_spec=pltpu.PrefetchScalarGridSpec(
            num_scalar_prefetch=1,
            grid=(length // QB,),
            in_specs=[
                pl.BlockSpec((QB, features), lambda i, spot: (i, 0)),
                pl.BlockSpec(weights.shape, lambda i, spot: (0, 0, 0)),
                pl.BlockSpec((1, width), lambda i, spot: (0, 0)),
            ],
            out_specs=(
                pl.BlockSpec((QB, width), lambda i, spot: (i, 0)),
                pl.BlockSpec((features, width), lambda i, spot: (0, 0)),
            ),
        ),
        cost_estimate=pl.CostEstimate(
            flops=2 * length * features * width, transcendentals=0, bytes_accessed=2 * length * (features + width)
        ),
        compiler_params=pltpu.CompilerParams(dimension_semantics=("arbitrary",)),
    )(spot, tokens, weights, bias)


def feed_forward_kernel(x_ref, up_ref, down_ref, bias_ref, act_ref, slope_ref, sum_ref):
    @pl.when(pl.program_id(0) == 0)
    def _():
        sum_ref[...] = jnp.zeros_like(sum_ref)

    up = piece_rows(up_ref)
    down = piece_rows(down_ref)
    for r in range(x_ref.shape[0] // QB):
        rows = slice(r * QB, (r + 1) * QB)
        hidden = mm(x_ref[rows, :], up) + bias_ref[0]
        area = 0.5 * (1.0 + lax.erf(hidden * (2.0**-0.5)))
        activated = (hidden * area).astype(BF)
        act_ref[rows, :] = activated
        slope_ref[rows, :] = (area + hidden * jnp.exp(-0.5 * hidden * hidden) * ((2.0 * jnp.pi) ** -0.5)).astype(BF)
        sum_ref[rows, :] += mm_nt(activated, down)


def feed_forward(x, weights, bias):
    length, features = x.shape
    dp, parts, cut, _ = weights.shape
    units = bias.shape[-1]
    piece = (dp, 1, cut, units)
    return pl.pallas_call(
        feed_forward_kernel,
        name="feed_forward",
        out_shape=(
            jax.ShapeDtypeStruct((length, parts * units), BF),
            jax.ShapeDtypeStruct((length, parts * units), BF),
            jax.ShapeDtypeStruct((length, features), F32),
        ),
        grid=(parts,),
        in_specs=[
            pl.BlockSpec((length, features), lambda t: (0, 0)),
            pl.BlockSpec(piece, lambda t: (0, t, 0, 0)),
            pl.BlockSpec(piece, lambda t: (0, t, 0, 1)),
            pl.BlockSpec((1, 1, units), lambda t: (t, 0, 0)),
        ],
        out_specs=(
            pl.BlockSpec((length, units), lambda t: (0, t)),
            pl.BlockSpec((length, units), lambda t: (0, t)),
            pl.BlockSpec((length, features), lambda t: (0, 0)),
        ),
        cost_estimate=pl.CostEstimate(
            flops=4 * length * features * parts * units,
            transcendentals=2 * length * parts * units,
            bytes_accessed=length * (parts * units * 4 + features * 6),
        ),
        compiler_params=pltpu.CompilerParams(dimension_semantics=("arbitrary",)),
    )(x, weights, weights, bias)


def feed_forward_backward_kernel(
    grad_ref, x_ref, act_ref, slope_ref, up_ref, down_ref, pack_ref, back_ref, bias_ref, xt_ref, gt_ref, gh_ref
):
    @pl.when(pl.program_id(0) == 0)
    def _():
        back_ref[...] = jnp.zeros_like(back_ref)
        xt_ref[...] = x_ref[...].T
        gt_ref[...] = grad_ref[...].T

    up = piece_rows(up_ref)
    down = piece_rows(down_ref)
    total = jnp.zeros((1, act_ref.shape[1]), F32)
    for r in range(x_ref.shape[0] // QB):
        rows = slice(r * QB, (r + 1) * QB)
        grad_hidden = (mm(grad_ref[rows, :], down) * slope_ref[rows, :].astype(F32)).astype(BF)
        gh_ref[rows, :] = grad_hidden
        total = total + jnp.sum(grad_hidden.astype(F32), axis=0, keepdims=True)
        back_ref[rows, :] += mm_nt(grad_hidden, up)
    bias_ref[0] = total
    units = act_ref.shape[1]
    split = (pack_ref.shape[0], pack_ref.shape[2], units)
    pack_ref[:, 0, :, 0:units] = mm(xt_ref[...], gh_ref[...]).astype(BF).reshape(split)
    pack_ref[:, 0, :, units : 2 * units] = mm(gt_ref[...], act_ref[...]).astype(BF).reshape(split)


def feed_forward_backward(grad, x, act, slope, weights):
    length, features = x.shape
    dp, parts, cut, width = weights.shape
    units = act.shape[1] // parts
    piece = (dp, 1, cut, units)
    whole = pl.BlockSpec((length, features), lambda t: (0, 0))
    part = pl.BlockSpec((length, units), lambda t: (0, t))
    return pl.pallas_call(
        feed_forward_backward_kernel,
        name="feed_forward_backward",
        out_shape=(
            jax.ShapeDtypeStruct((dp, parts, cut, width), BF),
            jax.ShapeDtypeStruct((length, features), F32),
            jax.ShapeDtypeStruct((parts, 1, units), F32),
        ),
        grid=(parts,),
        in_specs=[
            whole,
            whole,
            part,
            part,
            pl.BlockSpec(piece, lambda t: (0, t, 0, 0)),
            pl.BlockSpec(piece, lambda t: (0, t, 0, 1)),
        ],
        out_specs=(
            pl.BlockSpec((dp, 1, cut, 2 * units), lambda t: (0, t, 0, 0)),
            whole,
            pl.BlockSpec((1, 1, units), lambda t: (t, 0, 0)),
        ),
        scratch_shapes=[
            pltpu.VMEM((features, length), BF),
            pltpu.VMEM((features, length), BF),
            pltpu.VMEM((length, units), BF),
        ],
        cost_estimate=pl.CostEstimate(
            flops=8 * length * features * parts * units,
            transcendentals=0,
            bytes_accessed=length * (parts * units * 4 + features * 8) + dp * parts * cut * width * 4,
        ),
        compiler_params=pltpu.CompilerParams(dimension_semantics=("arbitrary",)),
    )(grad, x, act, slope, weights, weights)


def output_gradient_kernel(grad_ref, context_ref, _, pack_ref, full_ref):
    part = pl.program_id(0)
    columns = context_ref.shape[1] // 4

    @pl.when(part == 0)
    def _():
        full_ref[...] = mm(grad_ref[...].T, context_ref[...])

    split = (pack_ref.shape[0], pack_ref.shape[2], pack_ref.shape[3])
    for t in range(4):

        @pl.when(part == t)
        def _():
            at = (t % 2 * 2 + t // 2) * columns
            piece = full_ref[:, at : at + columns]
            rest = jnp.zeros((piece.shape[0], split[2] - columns), F32)
            pack_ref[:, 0] = jnp.concatenate([piece, rest], axis=1).astype(BF).reshape(split)


def output_gradient(grad, context, pack):
    length, features = grad.shape
    dp, parts, cut, width = pack.shape
    whole = pl.BlockSpec((length, features), lambda t: (0, 0))
    return pl.pallas_call(
        output_gradient_kernel,
        name="output_gradient",
        out_shape=jax.ShapeDtypeStruct(pack.shape, BF),
        grid=(parts,),
        in_specs=[whole, whole, pl.BlockSpec(memory_space=pl.ANY)],
        out_specs=pl.BlockSpec((dp, 1, cut, PAIR * 2), lambda t: (0, t, 0, width // (PAIR * 2) - 1)),
        scratch_shapes=[pltpu.VMEM((features, features), F32)],
        input_output_aliases={2: 0},
        cost_estimate=pl.CostEstimate(
            flops=2 * length * features * features, transcendentals=0, bytes_accessed=length * features * 4
        ),
        compiler_params=pltpu.CompilerParams(dimension_semantics=("arbitrary",)),
    )(grad, context, pack)


def make_per_device(dp):
    bits = dp.bit_length() - 1
    assert dp == 1 << bits

    def per_device(
        tokens,
        segment_ids,
        w_query,
        w_key,
        w_value,
        w_out,
        b_query,
        b_value,
        w_up,
        w_down,
        b_up,
        b_out,
        gain_one,
        shift_one,
        b_down,
        gain_two,
        shift_two,
        cotangent,
    ):
        place = lax.axis_index("tensor")
        depth = lax.axis_index("dp")
        across = place // 2
        core = place % 2
        _, quarter, features = tokens.shape
        cut, columns = w_query.shape
        units = w_up.shape[1]
        half = 2 * columns
        pairs = half // PAIR
        first_core = core == 0
        first_chip = across == 0
        tiled = cut % 16 == 0
        groups = (dp, cut) if tiled else (1, dp * cut)

        def swap_chips(value):
            return lax.ppermute(value, "tensor", [(0, 2), (2, 0), (1, 3), (3, 1)])

        def swap_cores(value):
            return lax.ppermute(value, "tensor", [(0, 1), (1, 0), (2, 3), (3, 2)])

        def swap_bit(value, b):
            return lax.ppermute(value, "dp", [(i, i ^ (1 << b)) for i in range(dp)])

        def bit_of(b):
            return (depth >> b) & 1

        def in_order(flag, mine, other, axis):
            return jnp.stack([jnp.where(flag, mine, other), jnp.where(flag, other, mine)], axis=axis)

        def mine_of(value, index, axis):
            return lax.dynamic_index_in_dim(value, index, axis, keepdims=False)

        attention_pack = jnp.concatenate([w_query, w_key, w_value], axis=1)
        if tiled:
            gathered = jnp.stack([attention_pack, swap_chips(attention_pack)])
            for b in reversed(range(bits)):
                gathered = jnp.concatenate([gathered, swap_bit(gathered, b)])
            spot = jnp.stack([depth, across]).astype(jnp.int32)
        else:
            gathered = lax.all_gather(attention_pack, BOTH, axis=0).reshape(dp, 2, 2, cut, 3 * columns)
            gathered = mine_of(gathered, core, 2).transpose(1, 0, 2, 3).reshape(2, dp * cut, 3 * columns)
            spot = jnp.zeros((2,), jnp.int32)

        tokens_own = in_order(first_chip, mine_of(tokens, across, 0), swap_chips(mine_of(tokens, 1 - across, 0)), 0)
        tokens_full = in_order(first_core, tokens_own, swap_cores(tokens_own), 1).reshape(4 * quarter, features)
        tokens_own = tokens_own.reshape(2 * quarter, features)

        small = [b_query, b_value, b_up, b_out, gain_one, shift_one, b_down, gain_two, shift_two]
        sizes = [v.size for v in small]
        lanes = -(-sum(sizes) // PAIR) * PAIR
        packed = jnp.concatenate([v.reshape(-1) for v in small])
        small_all = jnp.pad(packed, (0, lanes - packed.size)).reshape(1, lanes)
        small_all = in_order(first_chip, small_all, swap_chips(small_all), 0)
        for b in range(bits):
            small_all = in_order(bit_of(b) == 0, small_all, swap_bit(small_all, b), 0)
            small_all = small_all.reshape(2 << b, 2, 1, lanes)
        core_bias = small_all[:, :, 0, : sizes[0] + sizes[1]].reshape(dp, 2, 2, *b_query.shape).astype(F32)
        core_bias = core_bias.transpose(2, 1, 3, 0, 4).reshape(2, pairs, PAIR)
        bias_mine = jnp.stack([core_bias[0], jnp.zeros((pairs, PAIR), F32), core_bias[1]], axis=1).reshape(1, 3 * half)
        small_all = in_order(first_core, small_all, swap_cores(small_all), 2).reshape(dp, 4, lanes)
        pieces = []
        offset = 0
        for v, size in zip(small, sizes):
            piece = small_all[:, :, offset : offset + size].astype(F32)
            offset += size
            if v.ndim == 2:
                pieces.append(piece.reshape(dp, 4, *v.shape).transpose(1, 2, 0, 3))
            else:
                pieces.append(piece.reshape(-1))
        _, _, bias_up, out_bias, gain1, shift1, down_bias, gain2, shift2 = pieces
        bias_up = bias_up.reshape(4, 1, units)

        spare = jnp.zeros((cut, 2 * PAIR - columns), BF)
        other_pack = jnp.concatenate([w_up, w_down.T, w_out.T, spare], axis=1)
        width = other_pack.shape[1]
        others = lax.all_gather(other_pack, BOTH, axis=0).reshape(dp, 4, cut, width)
        if not tiled:
            others = others.transpose(1, 0, 2, 3).reshape(1, 4, dp * cut, width)

        cotangent_own = in_order(
            first_chip,
            mine_of(cotangent, across, 0),
            swap_chips(mine_of(cotangent, 1 - across, 0).astype(BF)).astype(F32),
            0,
        ).reshape(2 * quarter, features)
        lo, hi, bounds = segment_bounds(mine_of(segment_ids, across, 0))

        qkv, w_qkv = project(tokens_full, gathered, bias_mine, spot)
        heads_out, lse = attention_forward(qkv, lo, hi, bounds)

        by_core = heads_out.reshape(2, 2, quarter, half)
        kept = mine_of(by_core, core, 1)
        got = swap_cores(mine_of(by_core, 1 - core, 1))
        context = in_order(first_core, kept, got, 2).reshape(2 * quarter, 2 * half)

        w_out_t = (
            others[..., 2 * units : 2 * units + columns]
            .reshape(groups[0], 2, 2, groups[1], columns)
            .transpose(0, 3, 2, 1, 4)
            .reshape(features, features)
        )
        summed = tokens_own.astype(F32) + mm_nt(context, w_out_t) + out_bias
        hat1, inverse1 = statistics(summed)
        normed = hat1 * gain1 + shift1
        normed_low = normed.astype(BF)
        activated, slope, branch = feed_forward(normed_low, others, bias_up)
        hat2, inverse2 = statistics(normed + branch + down_bias)
        out_own = (hat2 * gain2 + shift2).reshape(2, quarter, features)

        def send_back(value):
            kept_part = mine_of(value, across, 0)
            got_part = swap_chips(mine_of(value, 1 - across, 0).astype(BF)).astype(F32)
            return in_order(first_chip, kept_part, got_part, 0)

        layer_out = send_back(out_own)

        grad_z = norm_backward(cotangent_own, hat2, inverse2, gain2)
        grad_branch = grad_z.astype(BF)
        pack, back, grad_bias_up = feed_forward_backward(grad_branch, normed_low, activated, slope, others)
        grad_normed = grad_z + back
        grad_summed = norm_backward(grad_normed, hat1, inverse1, gain1)
        grad_attended = grad_summed.astype(BF)
        pack = output_gradient(grad_attended, context, pack)
        if not tiled:
            pack = pack.reshape(4, dp, cut, width).transpose(1, 0, 2, 3)
        others_mine = lax.psum_scatter(pack.reshape(4 * dp, cut, width), BOTH, scatter_dimension=0, tiled=False)

        grad_context = mm(grad_attended, w_out_t).astype(BF).reshape(2, quarter, 2, half)
        kept = mine_of(grad_context, core, 2)
        got = swap_cores(mine_of(grad_context, 1 - core, 2))
        grad_heads = in_order(first_core, kept, got, 1).reshape(4 * quarter, half)

        grad_qkv = attention_backward(qkv, grad_heads, heads_out, lse, lo, hi, bounds)
        part = mm_nt(grad_qkv, w_qkv).reshape(2, 2, quarter, features)
        part_kept = mine_of(part, core, 1)
        part_got = swap_cores(mine_of(part, 1 - core, 1).astype(BF))
        grad_tokens = send_back(grad_summed.reshape(2, quarter, features) + part_kept + part_got.astype(F32))

        def halve(value, flag, swap, axis, kind):
            kept_half = mine_of(value, flag, axis)
            sent_half = mine_of(value, 1 - flag, axis)
            return (kept_half.astype(F32) + swap(sent_half).astype(F32)).astype(kind)

        grad_w = mm_tn(tokens_full, grad_qkv).astype(BF).reshape(dp, cut, 3 * half)
        for b in range(bits):
            grad_w = halve(grad_w.reshape(-1, 2, cut, 3 * half), bit_of(b), lambda v: swap_bit(v, b), 1, BF)
        grad_w = (
            grad_w.reshape(cut, pairs, 3, PAIR).transpose(0, 2, 1, 3).reshape(cut, 3, 2, columns).transpose(2, 0, 1, 3)
        )
        grad_w = halve(grad_w.reshape(2, cut, 3 * columns), across, swap_chips, 0, F32)

        bias_grads = jnp.sum(grad_qkv.astype(F32), axis=0).reshape(pairs, 3, PAIR)

        def matrix_small(value, like):
            return value.reshape(2, 2, like.shape[0], dp, like.shape[1]).transpose(3, 0, 1, 2, 4).reshape(dp, 2, 2, -1)

        def head_small(value, like):
            value = value.reshape(2, columns)
            zero = jnp.zeros_like(value)
            both = [jnp.where(first_core, value, zero), jnp.where(first_core, zero, value)]
            return matrix_small(jnp.stack(both, axis=1), like)

        def vector_small(value):
            return value.reshape(dp, 2, 2, -1)

        small_grads = jnp.concatenate(
            [
                head_small(bias_grads[:, 0], b_query),
                head_small(bias_grads[:, 2], b_value),
                matrix_small(grad_bias_up, b_up),
                vector_small(jnp.sum(grad_summed, axis=0)),
                vector_small(jnp.sum(grad_normed * hat1, axis=0)),
                vector_small(jnp.sum(grad_normed, axis=0)),
                vector_small(jnp.sum(grad_z, axis=0)),
                vector_small(jnp.sum(cotangent_own * hat2, axis=0)),
                vector_small(jnp.sum(cotangent_own, axis=0)),
            ],
            axis=3,
        )
        small_grads = jnp.pad(small_grads, ((0, 0), (0, 0), (0, 0), (0, lanes - small_grads.shape[3])))
        small_grads = halve(small_grads, core, swap_cores, 2, F32)
        for b in range(bits):
            small_grads = halve(small_grads.reshape(-1, 2, 2, lanes), bit_of(b), lambda v: swap_bit(v, b), 1, F32)
        small_grads = halve(small_grads.reshape(2, lanes), across, swap_chips, 0, F32)

        others_mine = others_mine.astype(F32)
        small_out = []
        offset = 0
        for v, size in zip(small, sizes):
            small_out.append(small_grads[offset : offset + size].reshape(v.shape))
            offset += size
        return (
            layer_out,
            grad_tokens,
            grad_w[:, :columns],
            grad_w[:, columns : 2 * columns],
            grad_w[:, 2 * columns :],
            others_mine[:, 2 * units : 2 * units + columns].T,
            small_out[0],
            small_out[1],
            others_mine[:, :units],
            others_mine[:, units : 2 * units].T,
            small_out[2],
            small_out[3],
            small_out[4],
            small_out[5],
            small_out[6],
            small_out[7],
            small_out[8],
        )

    return per_device


def solution(mesh):
    rows = P("dp", "tensor", None)
    split = P("dp", "tensor")
    turned = P("tensor", "dp")
    vector = P(("dp", "tensor"))
    in_specs = (rows, P("dp", None), split, split, split, turned, turned, turned, split, turned, turned)
    in_specs += (vector,) * 6 + (rows,)
    out_specs = (rows, rows, split, split, split, turned, turned, turned, split, turned, turned)
    out_specs += (vector,) * 6
    return jax.shard_map(
        make_per_device(mesh.shape["dp"]), mesh=mesh, in_specs=in_specs, out_specs=out_specs, check_vma=False
    )
```

```python
import jax
import jax.numpy as jnp
from jax import lax
from jax.experimental import pallas as pl
from jax.experimental.pallas import tpu as pltpu
from jax.sharding import PartitionSpec as P

HD = 64
PAIR = 2 * HD
SEGS = 12
QB = 512
KB = 256
RB = 256
NEG = -1e30
LIMIT = 50.0
GAP = 256.0
FREE = SEGS + 1
EXTRA = 16
EPS = 1e-12
BF = jnp.bfloat16
F32 = jnp.float32
BOTH = ("dp", "tensor")
NT = (((1,), (1,)), ((), ()))


def own_lanes(shape, h):
    lane = lax.broadcasted_iota(jnp.int32, shape, 1)
    return (lane < HD) if h % 2 == 0 else (lane >= HD)


def with_column(base, column, h):
    lane = lax.broadcasted_iota(jnp.int32, base.shape, 1) - (HD if h % 2 == 0 else 0)
    high = column.astype(BF).astype(F32)
    middle = (column - high).astype(BF).astype(F32)
    low = column - high - middle
    base = jnp.where(lane == FREE, high, base)
    base = jnp.where(lane == FREE + 1, middle, base)
    return jnp.where(lane == FREE + 2, low, base)


def fits(limit_ref, heads):
    largest = limit_ref[0, 0] * limit_ref[0, heads]
    for h in range(1, heads):
        largest = jnp.maximum(largest, limit_ref[0, h] * limit_ref[0, heads + h])
    return largest <= LIMIT * LIMIT


def attention_forward_kernel(
    lo_ref, hi_ref, limit_ref, bound_ref, q_ref, key_ref, val_ref, o_ref, lse_ref, acc_ref, top_ref
):
    row = pl.program_id(0)
    heads = key_ref.shape[1] // PAIR
    acc_ref[...] = jnp.zeros_like(acc_ref)
    plain = fits(limit_ref, heads)

    @pl.when(plain)
    def _():
        def step(kb, carry):
            there = pl.ds(pl.multiple_of(kb * KB, KB), KB)
            for h in range(heads):
                cols = slice(h * PAIR, (h + 1) * PAIR)
                scores = lax.dot_general(q_ref[:, cols], key_ref[there, cols], NT, preferred_element_type=F32)
                raised = jnp.exp(scores).astype(BF)
                acc_ref[:, cols] += jnp.dot(raised, val_ref[there, cols], preferred_element_type=F32)
            return carry

        lax.fori_loop(lo_ref[row], hi_ref[row], step, 0)
        top_ref[...] = jnp.zeros_like(top_ref)

    @pl.when(jnp.logical_not(plain))
    def _():
        start = bound_ref[0, 0:1, :].T
        end = bound_ref[0, 1:2, :].T
        top_ref[...] = jnp.full_like(top_ref, NEG)

        def step(kb, carry):
            base = pl.multiple_of(kb * KB, KB)
            there = pl.ds(base, KB)
            place = base + lax.broadcasted_iota(jnp.int32, (QB, KB), 1)
            valid = (place >= start) & (place < end)
            for h in range(heads):
                cols = slice(h * PAIR, (h + 1) * PAIR)
                scores = lax.dot_general(q_ref[:, cols], key_ref[there, cols], NT, preferred_element_type=F32)
                scores = jnp.where(valid, scores, NEG)
                before = top_ref[:, h : h + 1]
                top = jnp.maximum(before, jnp.max(scores, axis=1, keepdims=True))
                raised = jnp.exp(scores - top).astype(BF)
                acc_ref[:, cols] = jnp.exp(before - top) * acc_ref[:, cols] + jnp.dot(
                    raised, val_ref[there, cols], preferred_element_type=F32
                )
                top_ref[:, h : h + 1] = top
            return carry

        lax.fori_loop(lo_ref[row], hi_ref[row], step, 0)

    lse = top_ref[...]
    lane = lax.broadcasted_iota(jnp.int32, (QB, PAIR), 1)
    for p in range(heads // 2):
        both = []
        for h in (2 * p, 2 * p + 1):
            block = acc_ref[:, h * PAIR : (h + 1) * PAIR]
            at = SEGS + (HD if h % 2 == 0 else 0)
            total = block[:, at : at + 1]
            both.append(block / total)
            lse = jnp.where(lane == h, lse + jnp.log(total), lse)
        o_ref[:, p * PAIR : (p + 1) * PAIR] = jnp.where(lane < HD, both[0], both[1]).astype(BF)
    lse_ref[...] = lse


def attention_backward_kernel(
    lo_ref,
    hi_ref,
    limit_ref,
    bound_ref,
    lse_ref,
    q_ref,
    key_ref,
    val_ref,
    kt_ref,
    do_ref,
    o_ref,
    out_ref,
    dq_ref,
    dk_ref,
    dv_ref,
):
    row = pl.program_id(0)
    heads = key_ref.shape[1] // PAIR
    pairs = heads // 2

    @pl.when(row == 0)
    def _():
        dk_ref[...] = jnp.zeros_like(dk_ref)
        dv_ref[...] = jnp.zeros_like(dv_ref)

    here = pl.ds(pl.multiple_of(row * QB, QB), QB)
    q_parts, g_parts, q_score, g_score = [], [], [], []
    for p in range(pairs):
        cols = slice(p * PAIR, (p + 1) * PAIR)
        grad = do_ref[:, cols].astype(F32)
        product = grad * o_ref[:, cols].astype(F32)
        for h in (2 * p, 2 * p + 1):
            block = q_ref[:, h * PAIR : (h + 1) * PAIR].astype(F32)
            own = own_lanes(block.shape, h)
            inner = jnp.sum(jnp.where(own, product, 0.0), axis=1, keepdims=True)
            g_own = jnp.where(own, grad, 0.0)
            q_parts.append(jnp.where(own, block, 0.0).astype(BF))
            g_parts.append(g_own.astype(BF))
            q_score.append(with_column(block, -lse_ref[:, h : h + 1], h).astype(BF))
            g_score.append(with_column(g_own, -inner, h).astype(BF))
    dq_ref[...] = jnp.zeros_like(dq_ref)

    def sweep(masked):
        start = bound_ref[0, 0:1, :]
        end = bound_ref[0, 1:2, :]

        def step(kb, carry):
            base = pl.multiple_of(kb * KB, KB)
            there = pl.ds(base, KB)
            if masked:
                place = base + lax.broadcasted_iota(jnp.int32, (KB, QB), 0)
                valid = (place >= start) & (place < end)
            for p in range(pairs):
                cols = slice(p * PAIR, (p + 1) * PAIR)
                dk = dk_ref[there, cols]
                dv = dv_ref[there, cols]
                for h in (2 * p, 2 * p + 1):
                    keys = key_ref[there, h * PAIR : (h + 1) * PAIR]
                    vals = val_ref[there, h * PAIR : (h + 1) * PAIR]
                    scores = lax.dot_general(keys, q_score[h], NT, preferred_element_type=F32)
                    if masked:
                        scores = jnp.where(valid, scores, NEG)
                    weights = jnp.exp(scores)
                    grad_scores = weights * lax.dot_general(vals, g_score[h], NT, preferred_element_type=F32)
                    grad_scores = grad_scores.astype(BF)
                    dv = dv + jnp.dot(weights.astype(BF), g_parts[h], preferred_element_type=F32)
                    dk = dk + jnp.dot(grad_scores, q_parts[h], preferred_element_type=F32)
                    rows = slice(h * HD, (h + 1) * HD)
                    dq_ref[rows, :] += jnp.dot(kt_ref[rows, there], grad_scores, preferred_element_type=F32)
                dk_ref[there, cols] = dk
                dv_ref[there, cols] = dv
            return carry

        lax.fori_loop(lo_ref[row], hi_ref[row], step, 0)

    plain = fits(limit_ref, heads)
    pl.when(plain)(lambda: sweep(False))
    pl.when(jnp.logical_not(plain))(lambda: sweep(True))
    for p in range(pairs):
        cols = slice(p * PAIR, (p + 1) * PAIR)
        out_ref[here, 3 * p * PAIR : (3 * p + 1) * PAIR] = (dq_ref[cols, :] * HD ** (-0.5)).T.astype(BF)

    @pl.when(row == pl.num_programs(0) - 1)
    def _():
        for p in range(pairs):
            cols = slice(p * PAIR, (p + 1) * PAIR)
            out_ref[:, (3 * p + 1) * PAIR : (3 * p + 2) * PAIR] = dk_ref[:, cols].astype(BF)
            out_ref[:, (3 * p + 2) * PAIR : (3 * p + 3) * PAIR] = dv_ref[:, cols].astype(BF)


def attention_forward(operands, limits, segments):
    queries, keys, values, _ = operands
    lo, hi, bounds = segments[:3]
    length, wide = keys.shape
    heads = wide // PAIR
    whole = pl.BlockSpec((length, wide), lambda i, lo, hi: (0, 0))
    return pl.pallas_call(
        attention_forward_kernel,
        name="attention_forward",
        out_shape=(
            jax.ShapeDtypeStruct((length, heads * HD), BF),
            jax.ShapeDtypeStruct((length, PAIR), F32),
        ),
        grid_spec=pltpu.PrefetchScalarGridSpec(
            num_scalar_prefetch=2,
            grid=(length // QB,),
            in_specs=[
                pl.BlockSpec(memory_space=pltpu.SMEM),
                pl.BlockSpec((1, 2, QB), lambda i, lo, hi: (i, 0, 0)),
                pl.BlockSpec((QB, wide), lambda i, lo, hi: (i, 0)),
                whole,
                whole,
            ],
            out_specs=(
                pl.BlockSpec((QB, heads * HD), lambda i, lo, hi: (i, 0)),
                pl.BlockSpec((QB, PAIR), lambda i, lo, hi: (i, 0)),
            ),
            scratch_shapes=[pltpu.VMEM((QB, wide), F32), pltpu.VMEM((QB, PAIR), F32)],
        ),
        cost_estimate=pl.CostEstimate(
            flops=length * length * wide * 2,
            transcendentals=length * length * heads,
            bytes_accessed=keys.size * 7,
        ),
        compiler_params=pltpu.CompilerParams(dimension_semantics=("arbitrary",)),
    )(lo, hi, limits, bounds, queries, keys, values)


def attention_backward(operands, grad, out, lse, limits, segments):
    queries, keys, values, turned = operands
    lo, hi, bounds = segments[:3]
    length, wide = keys.shape
    heads = wide // PAIR
    width = heads * HD
    whole = pl.BlockSpec((length, wide), lambda i, lo, hi: (0, 0))
    rows = pl.BlockSpec((QB, width), lambda i, lo, hi: (i, 0))
    return pl.pallas_call(
        attention_backward_kernel,
        name="attention_backward",
        out_shape=jax.ShapeDtypeStruct((length, 3 * width), BF),
        grid_spec=pltpu.PrefetchScalarGridSpec(
            num_scalar_prefetch=2,
            grid=(length // QB,),
            in_specs=[
                pl.BlockSpec(memory_space=pltpu.SMEM),
                pl.BlockSpec((1, 2, QB), lambda i, lo, hi: (i, 0, 0)),
                pl.BlockSpec((QB, PAIR), lambda i, lo, hi: (i, 0)),
                pl.BlockSpec((QB, wide), lambda i, lo, hi: (i, 0)),
                whole,
                whole,
                pl.BlockSpec((width, length), lambda i, lo, hi: (0, 0)),
                rows,
                rows,
            ],
            out_specs=pl.BlockSpec((length, 3 * width), lambda i, lo, hi: (0, 0)),
            scratch_shapes=[
                pltpu.VMEM((width, QB), F32),
                pltpu.VMEM((length, width), F32),
                pltpu.VMEM((length, width), F32),
            ],
        ),
        cost_estimate=pl.CostEstimate(
            flops=length * length * wide * 5,
            transcendentals=length * length * heads,
            bytes_accessed=keys.size * 11,
        ),
        compiler_params=pltpu.CompilerParams(dimension_semantics=("arbitrary",)),
    )(lo, hi, limits, bounds, lse, queries, keys, values, turned, grad, out)


def segment_bounds(segments):
    length = segments.shape[0]
    names = jnp.arange(SEGS, dtype=jnp.int32)[:, None]
    counts = jnp.sum((segments[None, :] == names).astype(jnp.int32), axis=1, keepdims=True)
    start = jnp.sum(jnp.where(segments[None, :] > names, counts, 0), axis=0)
    end = jnp.sum(jnp.where(segments[None, :] >= names, counts, 0), axis=0)
    start = start.reshape(length // QB, QB)
    end = end.reshape(length // QB, QB)
    lo = start[:, 0] // KB
    hi = (end[:, -1] + (KB - 1)) // KB
    lane = jnp.arange(PAIR, dtype=jnp.int32)[None, :] % HD
    same = lane == segments[:, None]
    pattern = jnp.where((lane < SEGS) & same | (lane >= SEGS) & (lane < FREE + 3), 1.0, 0.0).astype(BF)
    qpattern = jnp.where(lane == SEGS, -GAP, jnp.where(same, GAP, 0.0)).astype(BF)
    return lo, hi, jnp.stack([start, end], axis=1), pattern, qpattern


def statistics(rows):
    centred = rows - jnp.mean(rows, axis=-1, keepdims=True)
    inverse = lax.rsqrt(jnp.mean(centred * centred, axis=-1, keepdims=True) + EPS)
    return centred * inverse, inverse


def norm_backward(grad, hat, inverse, gain):
    scaled = grad * gain
    return inverse * (
        scaled
        - jnp.mean(scaled, axis=-1, keepdims=True)
        - hat * jnp.mean(scaled * hat, axis=-1, keepdims=True)
    )


def mm(a, b):
    return lax.dot_general(a, b, (((1,), (0,)), ((), ())), preferred_element_type=F32)


def mm_nt(a, b):
    return lax.dot_general(a, b, NT, preferred_element_type=F32)


def mm_tn(a, b):
    return lax.dot_general(a, b, (((0,), (0,)), ((), ())), preferred_element_type=F32)


def piece_rows(ref):
    block = ref[:, 0]
    return block.reshape(block.shape[0] * block.shape[1], block.shape[2])


def project_kernel(
    spot_ref, tokens_ref, weights_ref, bias_ref, pattern_ref, qpattern_ref, q_ref, k_ref, v_ref, kt_ref, w_ref, limit_ref
):
    slots, cut, width = weights_ref.shape
    columns = width // 3
    bits = (slots // 2).bit_length() - 1
    pairs = 2 * columns // PAIR

    @pl.when(pl.program_id(0) == 0)
    def _():
        for d in range(slots // 2):
            other = d ^ spot_ref[0]
            slot = 0
            for b in range(bits):
                slot = slot * 2 + ((other >> b) & 1)
            first = weights_ref[slot * 2 + spot_ref[1]].astype(F32)
            second = weights_ref[slot * 2 + 1 - spot_ref[1]].astype(F32)
            for s in range(3):
                cols = slice(s * columns, (s + 1) * columns)
                joined = jnp.concatenate([first[:, cols], second[:, cols]], axis=1).astype(BF)
                for p in range(pairs):
                    at = (3 * p + s) * PAIR
                    w_ref[d * cut : (d + 1) * cut, at : at + PAIR] = joined[:, p * PAIR : (p + 1) * PAIR]
        limit_ref[...] = jnp.zeros_like(limit_ref)

    pattern = pattern_ref[...].astype(F32)
    qpattern = qpattern_ref[...].astype(F32)
    lane = lax.broadcasted_iota(jnp.int32, (8, PAIR), 1)[0:1, :]
    largest = limit_ref[...]
    for p in range(pairs):
        cols = slice(3 * p * PAIR, 3 * (p + 1) * PAIR)
        result = (mm(tokens_ref[...], w_ref[:, cols]) + bias_ref[:, cols]).astype(BF).astype(F32)
        queries = result[:, :PAIR] * HD ** (-0.5)
        keys = result[:, PAIR : 2 * PAIR]
        values = result[:, 2 * PAIR :]
        kt_ref[p * PAIR : (p + 1) * PAIR, :] = keys.astype(BF).T
        for h in (2 * p, 2 * p + 1):
            own = own_lanes(queries.shape, h)
            at = slice(h * PAIR, (h + 1) * PAIR)
            q_ref[:, at] = jnp.where(own, queries, qpattern).astype(BF)
            k_ref[:, at] = jnp.where(own, keys, pattern).astype(BF)
            v_ref[:, at] = jnp.where(own, values, pattern).astype(BF)
            for kind, part in enumerate((queries, keys)):
                square = jnp.sum(jnp.where(own, part * part, 0.0), axis=1, keepdims=True)
                peak = jnp.max(square, axis=0, keepdims=True)
                largest = jnp.where(lane == kind * 2 * pairs + h, jnp.maximum(largest, peak), largest)
    limit_ref[...] = largest


def project(tokens, weights, bias, spot, pattern, qpattern):
    length, features = tokens.shape
    width = 2 * weights.shape[2]
    wide = 2 * width // 3
    lanes = pl.BlockSpec((RB, PAIR), lambda i, spot: (i, 0))
    rows = pl.BlockSpec((RB, wide), lambda i, spot: (i, 0))
    return pl.pallas_call(
        project_kernel,
        name="project",
        out_shape=(
            jax.ShapeDtypeStruct((length, wide), BF),
            jax.ShapeDtypeStruct((length, wide), BF),
            jax.ShapeDtypeStruct((length, wide), BF),
            jax.ShapeDtypeStruct((width // 3, length), BF),
            jax.ShapeDtypeStruct((features, width), BF),
            jax.ShapeDtypeStruct((1, PAIR), F32),
        ),
        grid_spec=pltpu.PrefetchScalarGridSpec(
            num_scalar_prefetch=1,
            grid=(length // RB,),
            in_specs=[
                pl.BlockSpec((RB, features), lambda i, spot: (i, 0)),
                pl.BlockSpec(weights.shape, lambda i, spot: (0, 0, 0)),
                pl.BlockSpec((1, width), lambda i, spot: (0, 0)),
                lanes,
                lanes,
            ],
            out_specs=(
                rows,
                rows,
                rows,
                pl.BlockSpec((width // 3, RB), lambda i, spot: (0, i)),
                pl.BlockSpec((features, width), lambda i, spot: (0, 0)),
                pl.BlockSpec((1, PAIR), lambda i, spot: (0, 0)),
            ),
        ),
        cost_estimate=pl.CostEstimate(
            flops=2 * length * features * width, transcendentals=0, bytes_accessed=2 * length * (features + 3 * wide)
        ),
        compiler_params=pltpu.CompilerParams(dimension_semantics=("arbitrary",)),
    )(spot, tokens, weights, bias, pattern, qpattern)


def feed_forward_kernel(x_ref, up_ref, down_ref, bias_ref, act_ref, slope_ref, sum_ref):
    @pl.when(pl.program_id(0) == 0)
    def _():
        sum_ref[...] = jnp.zeros_like(sum_ref)

    up = piece_rows(up_ref)
    down = piece_rows(down_ref)
    for r in range(x_ref.shape[0] // RB):
        rows = slice(r * RB, (r + 1) * RB)
        hidden = mm(x_ref[rows, :], up) + bias_ref[0]
        area = 0.5 * (1.0 + lax.erf(hidden * (2.0**-0.5)))
        activated = (hidden * area).astype(BF)
        act_ref[rows, :] = activated
        slope_ref[rows, :] = (area + hidden * jnp.exp(-0.5 * hidden * hidden) * ((2.0 * jnp.pi) ** -0.5)).astype(BF)
        sum_ref[rows, :] += mm_nt(activated, down)


def feed_forward(x, weights, bias):
    length, features = x.shape
    dp, parts, cut, _ = weights.shape
    units = bias.shape[-1]
    piece = (dp, 1, cut, units)
    return pl.pallas_call(
        feed_forward_kernel,
        name="feed_forward",
        out_shape=(
            jax.ShapeDtypeStruct((length, parts * units), BF),
            jax.ShapeDtypeStruct((length, parts * units), BF),
            jax.ShapeDtypeStruct((length, features), F32),
        ),
        grid=(parts,),
        in_specs=[
            pl.BlockSpec((length, features), lambda t: (0, 0)),
            pl.BlockSpec(piece, lambda t: (0, t, 0, 0)),
            pl.BlockSpec(piece, lambda t: (0, t, 0, 1)),
            pl.BlockSpec((1, 1, units), lambda t: (t, 0, 0)),
        ],
        out_specs=(
            pl.BlockSpec((length, units), lambda t: (0, t)),
            pl.BlockSpec((length, units), lambda t: (0, t)),
            pl.BlockSpec((length, features), lambda t: (0, 0)),
        ),
        cost_estimate=pl.CostEstimate(
            flops=4 * length * features * parts * units,
            transcendentals=2 * length * parts * units,
            bytes_accessed=length * (parts * units * 4 + features * 6),
        ),
        compiler_params=pltpu.CompilerParams(dimension_semantics=("arbitrary",)),
    )(x, weights, weights, bias)


def feed_forward_backward_kernel(
    grad_ref, x_ref, act_ref, slope_ref, up_ref, down_ref, pack_ref, back_ref, bias_ref, xt_ref, gt_ref, gh_ref
):
    @pl.when(pl.program_id(0) == 0)
    def _():
        back_ref[...] = jnp.zeros_like(back_ref)
        xt_ref[...] = x_ref[...].T
        gt_ref[...] = grad_ref[...].T

    up = piece_rows(up_ref)
    down = piece_rows(down_ref)
    total = jnp.zeros((1, act_ref.shape[1]), F32)
    for r in range(x_ref.shape[0] // RB):
        rows = slice(r * RB, (r + 1) * RB)
        grad_hidden = (mm(grad_ref[rows, :], down) * slope_ref[rows, :].astype(F32)).astype(BF)
        gh_ref[rows, :] = grad_hidden
        total = total + jnp.sum(grad_hidden.astype(F32), axis=0, keepdims=True)
        back_ref[rows, :] += mm_nt(grad_hidden, up)
    bias_ref[0] = total
    units = act_ref.shape[1]
    split = (pack_ref.shape[0], pack_ref.shape[2], units)
    pack_ref[:, 0, :, 0:units] = mm(xt_ref[...], gh_ref[...]).astype(BF).reshape(split)
    pack_ref[:, 0, :, units : 2 * units] = mm(gt_ref[...], act_ref[...]).astype(BF).reshape(split)


def feed_forward_backward(grad, x, act, slope, weights):
    length, features = x.shape
    dp, parts, cut, width = weights.shape
    units = act.shape[1] // parts
    piece = (dp, 1, cut, units)
    whole = pl.BlockSpec((length, features), lambda t: (0, 0))
    part = pl.BlockSpec((length, units), lambda t: (0, t))
    return pl.pallas_call(
        feed_forward_backward_kernel,
        name="feed_forward_backward",
        out_shape=(
            jax.ShapeDtypeStruct((dp, parts, cut, width), BF),
            jax.ShapeDtypeStruct((length, features), F32),
            jax.ShapeDtypeStruct((parts, 1, units), F32),
        ),
        grid=(parts,),
        in_specs=[
            whole,
            whole,
            part,
            part,
            pl.BlockSpec(piece, lambda t: (0, t, 0, 0)),
            pl.BlockSpec(piece, lambda t: (0, t, 0, 1)),
        ],
        out_specs=(
            pl.BlockSpec((dp, 1, cut, 2 * units), lambda t: (0, t, 0, 0)),
            whole,
            pl.BlockSpec((1, 1, units), lambda t: (t, 0, 0)),
        ),
        scratch_shapes=[
            pltpu.VMEM((features, length), BF),
            pltpu.VMEM((features, length), BF),
            pltpu.VMEM((length, units), BF),
        ],
        cost_estimate=pl.CostEstimate(
            flops=8 * length * features * parts * units,
            transcendentals=0,
            bytes_accessed=length * (parts * units * 4 + features * 8) + dp * parts * cut * width * 4,
        ),
        compiler_params=pltpu.CompilerParams(dimension_semantics=("arbitrary",)),
    )(grad, x, act, slope, weights, weights)


def output_gradient_kernel(grad_ref, context_ref, _, pack_ref, full_ref):
    part = pl.program_id(0)
    columns = context_ref.shape[1] // 4

    @pl.when(part == 0)
    def _():
        full_ref[...] = mm(grad_ref[...].T, context_ref[...])

    split = (pack_ref.shape[0], pack_ref.shape[2], pack_ref.shape[3])
    for t in range(4):

        @pl.when(part == t)
        def _():
            at = (t % 2 * 2 + t // 2) * columns
            piece = full_ref[:, at : at + columns]
            rest = jnp.zeros((piece.shape[0], split[2] - columns), F32)
            pack_ref[:, 0] = jnp.concatenate([piece, rest], axis=1).astype(BF).reshape(split)


def output_gradient(grad, context, pack):
    length, features = grad.shape
    dp, parts, cut, width = pack.shape
    whole = pl.BlockSpec((length, features), lambda t: (0, 0))
    return pl.pallas_call(
        output_gradient_kernel,
        name="output_gradient",
        out_shape=jax.ShapeDtypeStruct(pack.shape, BF),
        grid=(parts,),
        in_specs=[whole, whole, pl.BlockSpec(memory_space=pl.ANY)],
        out_specs=pl.BlockSpec((dp, 1, cut, PAIR * 2), lambda t: (0, t, 0, width // (PAIR * 2) - 1)),
        scratch_shapes=[pltpu.VMEM((features, features), F32)],
        input_output_aliases={2: 0},
        cost_estimate=pl.CostEstimate(
            flops=2 * length * features * features, transcendentals=0, bytes_accessed=length * features * 4
        ),
        compiler_params=pltpu.CompilerParams(dimension_semantics=("arbitrary",)),
    )(grad, context, pack)


def make_per_device(dp):
    bits = dp.bit_length() - 1
    assert dp == 1 << bits

    def per_device(
        tokens,
        segment_ids,
        w_query,
        w_key,
        w_value,
        w_out,
        b_query,
        b_value,
        w_up,
        w_down,
        b_up,
        b_out,
        gain_one,
        shift_one,
        b_down,
        gain_two,
        shift_two,
        cotangent,
    ):
        place = lax.axis_index("tensor")
        depth = lax.axis_index("dp")
        across = place // 2
        core = place % 2
        _, quarter, features = tokens.shape
        cut, columns = w_query.shape
        units = w_up.shape[1]
        half = 2 * columns
        pairs = half // PAIR
        first_core = core == 0
        first_chip = across == 0
        tiled = cut % 16 == 0
        groups = (dp, cut) if tiled else (1, dp * cut)

        def swap_chips(value):
            return lax.ppermute(value, "tensor", [(0, 2), (2, 0), (1, 3), (3, 1)])

        def swap_cores(value):
            return lax.ppermute(value, "tensor", [(0, 1), (1, 0), (2, 3), (3, 2)])

        def swap_bit(value, b):
            return lax.ppermute(value, "dp", [(i, i ^ (1 << b)) for i in range(dp)])

        def bit_of(b):
            return (depth >> b) & 1

        def in_order(flag, mine, other, axis):
            return jnp.stack([jnp.where(flag, mine, other), jnp.where(flag, other, mine)], axis=axis)

        def mine_of(value, index, axis):
            return lax.dynamic_index_in_dim(value, index, axis, keepdims=False)

        attention_pack = jnp.concatenate([w_query, w_key, w_value], axis=1)
        if tiled:
            gathered = jnp.stack([attention_pack, swap_chips(attention_pack)])
            for b in reversed(range(bits)):
                before_last = gathered
                gathered = jnp.concatenate([gathered, swap_bit(gathered, b)])
            spot = jnp.stack([depth, across]).astype(jnp.int32)
        else:
            gathered = lax.all_gather(attention_pack, BOTH, axis=0).reshape(dp, 2, 2, cut, 3 * columns)
            gathered = mine_of(gathered, core, 2).transpose(1, 0, 2, 3).reshape(2, dp * cut, 3 * columns)
            spot = jnp.zeros((2,), jnp.int32)

        tokens_own = in_order(first_chip, mine_of(tokens, across, 0), swap_chips(mine_of(tokens, 1 - across, 0)), 0)
        tokens_full = in_order(first_core, tokens_own, swap_cores(tokens_own), 1).reshape(4 * quarter, features)
        tokens_own = tokens_own.reshape(2 * quarter, features)

        small = [b_query, b_value, b_up, b_out, gain_one, shift_one, b_down, gain_two, shift_two]
        sizes = [v.size for v in small]
        lanes = -(-sum(sizes) // PAIR) * PAIR
        packed = jnp.concatenate([v.reshape(-1) for v in small])
        small_all = jnp.pad(packed, (0, lanes - packed.size)).reshape(1, lanes)
        small_all = in_order(first_chip, small_all, swap_chips(small_all), 0)
        for b in range(bits):
            small_all = in_order(bit_of(b) == 0, small_all, swap_bit(small_all, b), 0)
            small_all = small_all.reshape(2 << b, 2, 1, lanes)
        core_bias = small_all[:, :, 0, : sizes[0] + sizes[1]].reshape(dp, 2, 2, *b_query.shape).astype(F32)
        core_bias = core_bias.transpose(2, 1, 3, 0, 4).reshape(2, pairs, PAIR)
        bias_mine = jnp.stack([core_bias[0], jnp.zeros((pairs, PAIR), F32), core_bias[1]], axis=1).reshape(1, 3 * half)
        small_all = in_order(first_core, small_all, swap_cores(small_all), 2).reshape(dp, 4, lanes)
        pieces = []
        offset = 0
        for v, size in zip(small, sizes):
            piece = small_all[:, :, offset : offset + size].astype(F32)
            offset += size
            if v.ndim == 2:
                pieces.append(piece.reshape(dp, 4, *v.shape).transpose(1, 2, 0, 3))
            else:
                pieces.append(piece.reshape(-1))
        _, _, bias_up, out_bias, gain1, shift1, down_bias, gain2, shift2 = pieces
        bias_up = bias_up.reshape(4, 1, units)

        spare = jnp.zeros((cut, 2 * PAIR - columns), BF)
        other_pack = jnp.concatenate([w_up, w_down.T, w_out.T, spare], axis=1)
        width = other_pack.shape[1]
        if tiled:
            other_pack, _ = lax.optimization_barrier((other_pack, before_last))
        others = lax.all_gather(other_pack, BOTH, axis=0).reshape(dp, 4, cut, width)
        if not tiled:
            others = others.transpose(1, 0, 2, 3).reshape(1, 4, dp * cut, width)

        cotangent_own = in_order(
            first_chip,
            mine_of(cotangent, across, 0),
            swap_chips(mine_of(cotangent, 1 - across, 0).astype(BF)).astype(F32),
            0,
        ).reshape(2 * quarter, features)
        segments = segment_bounds(mine_of(segment_ids, across, 0))

        *operands, w_qkv, limits = project(tokens_full, gathered, bias_mine, spot, *segments[3:])
        heads_out, lse = attention_forward(operands, limits, segments)

        by_core = heads_out.reshape(2, 2, quarter, half)
        kept = mine_of(by_core, core, 1)
        got = swap_cores(mine_of(by_core, 1 - core, 1))
        context = in_order(first_core, kept, got, 2).reshape(2 * quarter, 2 * half)

        w_out_t = (
            others[..., 2 * units : 2 * units + columns]
            .reshape(groups[0], 2, 2, groups[1], columns)
            .transpose(0, 3, 2, 1, 4)
            .reshape(features, features)
        )
        summed = tokens_own.astype(F32) + mm_nt(context, w_out_t) + out_bias
        hat1, inverse1 = statistics(summed)
        normed = hat1 * gain1 + shift1
        normed_low = normed.astype(BF)
        activated, slope, branch = feed_forward(normed_low, others, bias_up)
        hat2, inverse2 = statistics(normed + branch + down_bias)
        out_own = (hat2 * gain2 + shift2).reshape(2, quarter, features)

        def send_back(value):
            kept_part = mine_of(value, across, 0)
            got_part = swap_chips(mine_of(value, 1 - across, 0).astype(BF)).astype(F32)
            return in_order(first_chip, kept_part, got_part, 0)

        layer_out = send_back(out_own)

        grad_z = norm_backward(cotangent_own, hat2, inverse2, gain2)
        grad_branch = grad_z.astype(BF)
        pack, back, grad_bias_up = feed_forward_backward(grad_branch, normed_low, activated, slope, others)
        grad_normed = grad_z + back
        grad_summed = norm_backward(grad_normed, hat1, inverse1, gain1)
        grad_attended = grad_summed.astype(BF)
        pack = output_gradient(grad_attended, context, pack)
        if not tiled:
            pack = pack.reshape(4, dp, cut, width).transpose(1, 0, 2, 3)
        others_mine = lax.psum_scatter(pack.reshape(4 * dp, cut, width), BOTH, scatter_dimension=0, tiled=False)

        grad_context = mm(grad_attended, w_out_t).astype(BF).reshape(2, quarter, 2, half)
        kept = mine_of(grad_context, core, 2)
        got = swap_cores(mine_of(grad_context, 1 - core, 2))
        grad_heads = in_order(first_core, kept, got, 1).reshape(4 * quarter, half)

        grad_qkv = attention_backward(operands, grad_heads, heads_out, lse, limits, segments)
        part = mm_nt(grad_qkv, w_qkv).reshape(2, 2, quarter, features)
        part_kept = mine_of(part, core, 1)
        part_got = swap_cores(mine_of(part, 1 - core, 1).astype(BF))
        grad_tokens = send_back(grad_summed.reshape(2, quarter, features) + part_kept + part_got.astype(F32))

        def halve(value, flag, swap, axis, kind):
            kept_half = mine_of(value, flag, axis)
            sent_half = mine_of(value, 1 - flag, axis)
            return (kept_half.astype(F32) + swap(sent_half).astype(F32)).astype(kind)

        grad_w = mm_tn(tokens_full, grad_qkv).astype(BF).reshape(dp, cut, 3 * half)
        for b in range(bits):
            grad_w = halve(grad_w.reshape(-1, 2, cut, 3 * half), bit_of(b), lambda v: swap_bit(v, b), 1, BF)
        grad_w = (
            grad_w.reshape(cut, pairs, 3, PAIR).transpose(0, 2, 1, 3).reshape(cut, 3, 2, columns).transpose(2, 0, 1, 3)
        )
        grad_w = halve(grad_w.reshape(2, cut, 3 * columns), across, swap_chips, 0, F32)

        bias_grads = jnp.sum(grad_qkv.astype(F32), axis=0).reshape(pairs, 3, PAIR)

        def matrix_small(value, like):
            return value.reshape(2, 2, like.shape[0], dp, like.shape[1]).transpose(3, 0, 1, 2, 4).reshape(dp, 2, 2, -1)

        def head_small(value, like):
            value = value.reshape(2, columns)
            zero = jnp.zeros_like(value)
            both = [jnp.where(first_core, value, zero), jnp.where(first_core, zero, value)]
            return matrix_small(jnp.stack(both, axis=1), like)

        def vector_small(value):
            return value.reshape(dp, 2, 2, -1)

        small_grads = jnp.concatenate(
            [
                head_small(bias_grads[:, 0], b_query),
                head_small(bias_grads[:, 2], b_value),
                matrix_small(grad_bias_up, b_up),
                vector_small(jnp.sum(grad_summed, axis=0)),
                vector_small(jnp.sum(grad_normed * hat1, axis=0)),
                vector_small(jnp.sum(grad_normed, axis=0)),
                vector_small(jnp.sum(grad_z, axis=0)),
                vector_small(jnp.sum(cotangent_own * hat2, axis=0)),
                vector_small(jnp.sum(cotangent_own, axis=0)),
            ],
            axis=3,
        )
        small_grads = jnp.pad(small_grads, ((0, 0), (0, 0), (0, 0), (0, lanes - small_grads.shape[3])))
        small_grads = halve(small_grads, core, swap_cores, 2, F32)
        for b in range(bits):
            small_grads = halve(small_grads.reshape(-1, 2, 2, lanes), bit_of(b), lambda v: swap_bit(v, b), 1, F32)
        small_grads = halve(small_grads.reshape(2, lanes), across, swap_chips, 0, F32)

        others_mine = others_mine.astype(F32)
        small_out = []
        offset = 0
        for v, size in zip(small, sizes):
            small_out.append(small_grads[offset : offset + size].reshape(v.shape))
            offset += size
        return (
            layer_out,
            grad_tokens,
            grad_w[:, :columns],
            grad_w[:, columns : 2 * columns],
            grad_w[:, 2 * columns :],
            others_mine[:, 2 * units : 2 * units + columns].T,
            small_out[0],
            small_out[1],
            others_mine[:, :units],
            others_mine[:, units : 2 * units].T,
            small_out[2],
            small_out[3],
            small_out[4],
            small_out[5],
            small_out[6],
            small_out[7],
            small_out[8],
        )

    return per_device


def solution(mesh):
    rows = P("dp", "tensor", None)
    split = P("dp", "tensor")
    turned = P("tensor", "dp")
    vector = P(("dp", "tensor"))
    in_specs = (rows, P("dp", None), split, split, split, turned, turned, turned, split, turned, turned)
    in_specs += (vector,) * 6 + (rows,)
    out_specs = (rows, rows, split, split, split, turned, turned, turned, split, turned, turned)
    out_specs += (vector,) * 6
    return jax.shard_map(
        make_per_device(mesh.shape["dp"]), mesh=mesh, in_specs=in_specs, out_specs=out_specs, check_vma=False
    )
```

```python
import jax
import jax.numpy as jnp
from jax import lax
from jax.experimental import pallas as pl
from jax.experimental.pallas import tpu as pltpu
from jax.sharding import PartitionSpec as P


HD = 64
PAIR = 2 * HD
SEGS = 12
QB = 512
KB = 256
RB = 256
NEG = -1e30
LIMIT = 50.0
GAP = 256.0
FREE = SEGS + 1
EPS = 1e-12
BF = jnp.bfloat16
F32 = jnp.float32
BOTH = ("dp", "tensor")
NT = (((1,), (1,)), ((), ()))


def own_lanes(shape, h):
    lane = lax.broadcasted_iota(jnp.int32, shape, 1)
    return (lane < HD) if h % 2 == 0 else (lane >= HD)


def with_column(base, column, h):
    lane = lax.broadcasted_iota(jnp.int32, base.shape, 1) - (HD if h % 2 == 0 else 0)
    high = column.astype(BF).astype(F32)
    middle = (column - high).astype(BF).astype(F32)
    low = column - high - middle
    base = jnp.where(lane == FREE, high, base)
    base = jnp.where(lane == FREE + 1, middle, base)
    return jnp.where(lane == FREE + 2, low, base)


def fits(limit_ref, heads):
    largest = limit_ref[0, 0] * limit_ref[0, heads]
    for h in range(1, heads):
        largest = jnp.maximum(largest, limit_ref[0, h] * limit_ref[0, heads + h])
    return largest <= LIMIT * LIMIT


def attention_forward_kernel(
    lo_ref, hi_ref, limit_ref, bound_ref, q_ref, key_ref, val_ref, o_ref, lse_ref, acc_ref, top_ref
):
    row = pl.program_id(0)
    heads = key_ref.shape[1] // PAIR
    acc_ref[...] = jnp.zeros_like(acc_ref)
    plain = fits(limit_ref, heads)

    @pl.when(plain)
    def _():
        def step(kb, carry):
            there = pl.ds(pl.multiple_of(kb * KB, KB), KB)
            for h in range(heads):
                cols = slice(h * PAIR, (h + 1) * PAIR)
                scores = lax.dot_general(q_ref[:, cols], key_ref[there, cols], NT, preferred_element_type=F32)
                raised = jnp.exp(scores).astype(BF)
                acc_ref[:, cols] += jnp.dot(raised, val_ref[there, cols], preferred_element_type=F32)
            return carry

        lax.fori_loop(lo_ref[row], hi_ref[row], step, 0)
        top_ref[...] = jnp.zeros_like(top_ref)

    @pl.when(jnp.logical_not(plain))
    def _():
        start = bound_ref[0, 0:1, :].T
        end = bound_ref[0, 1:2, :].T
        top_ref[...] = jnp.full_like(top_ref, NEG)

        def step(kb, carry):
            base = pl.multiple_of(kb * KB, KB)
            there = pl.ds(base, KB)
            place = base + lax.broadcasted_iota(jnp.int32, (QB, KB), 1)
            valid = (place >= start) & (place < end)
            for h in range(heads):
                cols = slice(h * PAIR, (h + 1) * PAIR)
                scores = lax.dot_general(q_ref[:, cols], key_ref[there, cols], NT, preferred_element_type=F32)
                scores = jnp.where(valid, scores, NEG)
                before = top_ref[:, h : h + 1]
                top = jnp.maximum(before, jnp.max(scores, axis=1, keepdims=True))
                raised = jnp.exp(scores - top).astype(BF)
                acc_ref[:, cols] = jnp.exp(before - top) * acc_ref[:, cols] + jnp.dot(
                    raised, val_ref[there, cols], preferred_element_type=F32
                )
                top_ref[:, h : h + 1] = top
            return carry

        lax.fori_loop(lo_ref[row], hi_ref[row], step, 0)

    lse = top_ref[...]
    lane = lax.broadcasted_iota(jnp.int32, (QB, PAIR), 1)
    for p in range(heads // 2):
        both = []
        for h in (2 * p, 2 * p + 1):
            block = acc_ref[:, h * PAIR : (h + 1) * PAIR]
            at = SEGS + (HD if h % 2 == 0 else 0)
            total = block[:, at : at + 1]
            both.append(block / total)
            lse = jnp.where(lane == h, lse + jnp.log(total), lse)
        o_ref[:, p * PAIR : (p + 1) * PAIR] = jnp.where(lane < HD, both[0], both[1]).astype(BF)
    lse_ref[...] = lse


def attention_backward_kernel(
    lo_ref,
    hi_ref,
    limit_ref,
    bound_ref,
    lse_ref,
    q_ref,
    key_ref,
    val_ref,
    kt_ref,
    do_ref,
    o_ref,
    out_ref,
    dq_ref,
    dk_ref,
    dv_ref,
):
    row = pl.program_id(0)
    heads = key_ref.shape[1] // PAIR
    pairs = heads // 2

    @pl.when(row == 0)
    def _():
        dk_ref[...] = jnp.zeros_like(dk_ref)
        dv_ref[...] = jnp.zeros_like(dv_ref)

    here = pl.ds(pl.multiple_of(row * QB, QB), QB)
    q_parts, g_parts, q_score, g_score = [], [], [], []
    for p in range(pairs):
        cols = slice(p * PAIR, (p + 1) * PAIR)
        grad = do_ref[:, cols].astype(F32)
        product = grad * o_ref[:, cols].astype(F32)
        for h in (2 * p, 2 * p + 1):
            block = q_ref[:, h * PAIR : (h + 1) * PAIR].astype(F32)
            own = own_lanes(block.shape, h)
            inner = jnp.sum(jnp.where(own, product, 0.0), axis=1, keepdims=True)
            g_own = jnp.where(own, grad, 0.0)
            q_parts.append(jnp.where(own, block, 0.0).astype(BF))
            g_parts.append(g_own.astype(BF))
            q_score.append(with_column(block, -lse_ref[:, h : h + 1], h).astype(BF))
            g_score.append(with_column(g_own, -inner, h).astype(BF))
    dq_ref[...] = jnp.zeros_like(dq_ref)

    def sweep(masked):
        start = bound_ref[0, 0:1, :]
        end = bound_ref[0, 1:2, :]

        def step(kb, carry):
            base = pl.multiple_of(kb * KB, KB)
            there = pl.ds(base, KB)
            if masked:
                place = base + lax.broadcasted_iota(jnp.int32, (KB, QB), 0)
                valid = (place >= start) & (place < end)
            for p in range(pairs):
                cols = slice(p * PAIR, (p + 1) * PAIR)
                dk = dk_ref[there, cols]
                dv = dv_ref[there, cols]
                for h in (2 * p, 2 * p + 1):
                    keys = key_ref[there, h * PAIR : (h + 1) * PAIR]
                    vals = val_ref[there, h * PAIR : (h + 1) * PAIR]
                    scores = lax.dot_general(keys, q_score[h], NT, preferred_element_type=F32)
                    if masked:
                        scores = jnp.where(valid, scores, NEG)
                    weights = jnp.exp(scores)
                    grad_scores = weights * lax.dot_general(vals, g_score[h], NT, preferred_element_type=F32)
                    grad_scores = grad_scores.astype(BF)
                    dv = dv + jnp.dot(weights.astype(BF), g_parts[h], preferred_element_type=F32)
                    dk = dk + jnp.dot(grad_scores, q_parts[h], preferred_element_type=F32)
                    rows = slice(h * HD, (h + 1) * HD)
                    dq_ref[rows, :] += jnp.dot(kt_ref[rows, there], grad_scores, preferred_element_type=F32)
                dk_ref[there, cols] = dk
                dv_ref[there, cols] = dv
            return carry

        lax.fori_loop(lo_ref[row], hi_ref[row], step, 0)

    plain = fits(limit_ref, heads)
    pl.when(plain)(lambda: sweep(False))
    pl.when(jnp.logical_not(plain))(lambda: sweep(True))
    for p in range(pairs):
        cols = slice(p * PAIR, (p + 1) * PAIR)
        out_ref[here, 3 * p * PAIR : (3 * p + 1) * PAIR] = (dq_ref[cols, :] * HD ** (-0.5)).T.astype(BF)

    @pl.when(row == pl.num_programs(0) - 1)
    def _():
        for p in range(pairs):
            cols = slice(p * PAIR, (p + 1) * PAIR)
            out_ref[:, (3 * p + 1) * PAIR : (3 * p + 2) * PAIR] = dk_ref[:, cols].astype(BF)
            out_ref[:, (3 * p + 2) * PAIR : (3 * p + 3) * PAIR] = dv_ref[:, cols].astype(BF)


def attention_forward(operands, limits, segments):
    queries, keys, values, _ = operands
    lo, hi, bounds = segments[:3]
    length, wide = keys.shape
    heads = wide // PAIR
    whole = pl.BlockSpec((length, wide), lambda i, lo, hi: (0, 0))
    return pl.pallas_call(
        attention_forward_kernel,
        name="attention_forward",
        out_shape=(
            jax.ShapeDtypeStruct((length, heads * HD), BF),
            jax.ShapeDtypeStruct((length, PAIR), F32),
        ),
        grid_spec=pltpu.PrefetchScalarGridSpec(
            num_scalar_prefetch=2,
            grid=(length // QB,),
            in_specs=[
                pl.BlockSpec(memory_space=pltpu.SMEM),
                pl.BlockSpec((1, 2, QB), lambda i, lo, hi: (i, 0, 0)),
                pl.BlockSpec((QB, wide), lambda i, lo, hi: (i, 0)),
                whole,
                whole,
            ],
            out_specs=(
                pl.BlockSpec((QB, heads * HD), lambda i, lo, hi: (i, 0)),
                pl.BlockSpec((QB, PAIR), lambda i, lo, hi: (i, 0)),
            ),
            scratch_shapes=[pltpu.VMEM((QB, wide), F32), pltpu.VMEM((QB, PAIR), F32)],
        ),
        cost_estimate=pl.CostEstimate(
            flops=length * length * wide * 2,
            transcendentals=length * length * heads,
            bytes_accessed=keys.size * 7,
        ),
        compiler_params=pltpu.CompilerParams(dimension_semantics=("arbitrary",)),
    )(lo, hi, limits, bounds, queries, keys, values)


def attention_backward(operands, grad, out, lse, limits, segments):
    queries, keys, values, turned = operands
    lo, hi, bounds = segments[:3]
    length, wide = keys.shape
    heads = wide // PAIR
    width = heads * HD
    whole = pl.BlockSpec((length, wide), lambda i, lo, hi: (0, 0))
    rows = pl.BlockSpec((QB, width), lambda i, lo, hi: (i, 0))
    return pl.pallas_call(
        attention_backward_kernel,
        name="attention_backward",
        out_shape=jax.ShapeDtypeStruct((length, 3 * width), BF),
        grid_spec=pltpu.PrefetchScalarGridSpec(
            num_scalar_prefetch=2,
            grid=(length // QB,),
            in_specs=[
                pl.BlockSpec(memory_space=pltpu.SMEM),
                pl.BlockSpec((1, 2, QB), lambda i, lo, hi: (i, 0, 0)),
                pl.BlockSpec((QB, PAIR), lambda i, lo, hi: (i, 0)),
                pl.BlockSpec((QB, wide), lambda i, lo, hi: (i, 0)),
                whole,
                whole,
                pl.BlockSpec((width, length), lambda i, lo, hi: (0, 0)),
                rows,
                rows,
            ],
            out_specs=pl.BlockSpec((length, 3 * width), lambda i, lo, hi: (0, 0)),
            scratch_shapes=[
                pltpu.VMEM((width, QB), F32),
                pltpu.VMEM((length, width), F32),
                pltpu.VMEM((length, width), F32),
            ],
        ),
        cost_estimate=pl.CostEstimate(
            flops=length * length * wide * 5,
            transcendentals=length * length * heads,
            bytes_accessed=keys.size * 11,
        ),
        compiler_params=pltpu.CompilerParams(dimension_semantics=("arbitrary",)),
    )(lo, hi, limits, bounds, lse, queries, keys, values, turned, grad, out)


def segment_bounds(segments):
    length = segments.shape[0]
    names = jnp.arange(SEGS, dtype=jnp.int32)[:, None]
    counts = jnp.sum((segments[None, :] == names).astype(jnp.int32), axis=1, keepdims=True)
    start = jnp.sum(jnp.where(segments[None, :] > names, counts, 0), axis=0)
    end = jnp.sum(jnp.where(segments[None, :] >= names, counts, 0), axis=0)
    start = start.reshape(length // QB, QB)
    end = end.reshape(length // QB, QB)
    lo = start[:, 0] // KB
    hi = (end[:, -1] + (KB - 1)) // KB
    lane = jnp.arange(PAIR, dtype=jnp.int32)[None, :] % HD
    same = lane == segments[:, None]
    pattern = jnp.where((lane < SEGS) & same | (lane >= SEGS) & (lane < FREE + 3), 1.0, 0.0).astype(BF)
    qpattern = jnp.where(lane == SEGS, -GAP, jnp.where(same, GAP, 0.0)).astype(BF)
    return lo, hi, jnp.stack([start, end], axis=1), pattern, qpattern


def statistics(rows):
    centred = rows - jnp.mean(rows, axis=-1, keepdims=True)
    inverse = lax.rsqrt(jnp.mean(centred * centred, axis=-1, keepdims=True) + EPS)
    return centred * inverse, inverse


def norm_backward(grad, hat, inverse, gain):
    scaled = grad * gain
    return inverse * (
        scaled
        - jnp.mean(scaled, axis=-1, keepdims=True)
        - hat * jnp.mean(scaled * hat, axis=-1, keepdims=True)
    )


def mm(a, b):
    return lax.dot_general(a, b, (((1,), (0,)), ((), ())), preferred_element_type=F32)


def mm_nt(a, b):
    return lax.dot_general(a, b, NT, preferred_element_type=F32)


def mm_tn(a, b):
    return lax.dot_general(a, b, (((0,), (0,)), ((), ())), preferred_element_type=F32)


def piece_rows(ref):
    block = ref[:, 0]
    return block.reshape(block.shape[0] * block.shape[1], block.shape[2])


def project_kernel(
    spot_ref, tokens_ref, weights_ref, bias_ref, pattern_ref, qpattern_ref, q_ref, k_ref, v_ref, kt_ref, w_ref, limit_ref
):
    slots, cut, width = weights_ref.shape
    columns = width // 3
    bits = (slots // 2).bit_length() - 1
    pairs = 2 * columns // PAIR

    @pl.when(pl.program_id(0) == 0)
    def _():
        for d in range(slots // 2):
            other = d ^ spot_ref[0]
            slot = 0
            for b in range(bits):
                slot = slot * 2 + ((other >> b) & 1)
            first = weights_ref[slot * 2 + spot_ref[1]].astype(F32)
            second = weights_ref[slot * 2 + 1 - spot_ref[1]].astype(F32)
            for s in range(3):
                cols = slice(s * columns, (s + 1) * columns)
                joined = jnp.concatenate([first[:, cols], second[:, cols]], axis=1).astype(BF)
                for p in range(pairs):
                    at = (3 * p + s) * PAIR
                    w_ref[d * cut : (d + 1) * cut, at : at + PAIR] = joined[:, p * PAIR : (p + 1) * PAIR]
        limit_ref[...] = jnp.zeros_like(limit_ref)

    pattern = pattern_ref[...].astype(F32)
    qpattern = qpattern_ref[...].astype(F32)
    lane = lax.broadcasted_iota(jnp.int32, (8, PAIR), 1)[0:1, :]
    largest = limit_ref[...]
    for p in range(pairs):
        cols = slice(3 * p * PAIR, 3 * (p + 1) * PAIR)
        result = (mm(tokens_ref[...], w_ref[:, cols]) + bias_ref[:, cols]).astype(BF).astype(F32)
        queries = result[:, :PAIR] * HD ** (-0.5)
        keys = result[:, PAIR : 2 * PAIR]
        values = result[:, 2 * PAIR :]
        kt_ref[p * PAIR : (p + 1) * PAIR, :] = keys.astype(BF).T
        for h in (2 * p, 2 * p + 1):
            own = own_lanes(queries.shape, h)
            at = slice(h * PAIR, (h + 1) * PAIR)
            q_ref[:, at] = jnp.where(own, queries, qpattern).astype(BF)
            k_ref[:, at] = jnp.where(own, keys, pattern).astype(BF)
            v_ref[:, at] = jnp.where(own, values, pattern).astype(BF)
            for kind, part in enumerate((queries, keys)):
                square = jnp.sum(jnp.where(own, part * part, 0.0), axis=1, keepdims=True)
                peak = jnp.max(square, axis=0, keepdims=True)
                largest = jnp.where(lane == kind * 2 * pairs + h, jnp.maximum(largest, peak), largest)
    limit_ref[...] = largest


def project(tokens, weights, bias, spot, pattern, qpattern):
    length, features = tokens.shape
    width = 2 * weights.shape[2]
    wide = 2 * width // 3
    lanes = pl.BlockSpec((RB, PAIR), lambda i, spot: (i, 0))
    rows = pl.BlockSpec((RB, wide), lambda i, spot: (i, 0))
    return pl.pallas_call(
        project_kernel,
        name="project",
        out_shape=(
            jax.ShapeDtypeStruct((length, wide), BF),
            jax.ShapeDtypeStruct((length, wide), BF),
            jax.ShapeDtypeStruct((length, wide), BF),
            jax.ShapeDtypeStruct((width // 3, length), BF),
            jax.ShapeDtypeStruct((features, width), BF),
            jax.ShapeDtypeStruct((1, PAIR), F32),
        ),
        grid_spec=pltpu.PrefetchScalarGridSpec(
            num_scalar_prefetch=1,
            grid=(length // RB,),
            in_specs=[
                pl.BlockSpec((RB, features), lambda i, spot: (i, 0)),
                pl.BlockSpec(weights.shape, lambda i, spot: (0, 0, 0)),
                pl.BlockSpec((1, width), lambda i, spot: (0, 0)),
                lanes,
                lanes,
            ],
            out_specs=(
                rows,
                rows,
                rows,
                pl.BlockSpec((width // 3, RB), lambda i, spot: (0, i)),
                pl.BlockSpec((features, width), lambda i, spot: (0, 0)),
                pl.BlockSpec((1, PAIR), lambda i, spot: (0, 0)),
            ),
        ),
        cost_estimate=pl.CostEstimate(
            flops=2 * length * features * width, transcendentals=0, bytes_accessed=2 * length * (features + 3 * wide)
        ),
        compiler_params=pltpu.CompilerParams(dimension_semantics=("arbitrary",)),
    )(spot, tokens, weights, bias, pattern, qpattern)


def feed_forward_kernel(x_ref, up_ref, down_ref, bias_ref, act_ref, slope_ref, sum_ref):
    @pl.when(pl.program_id(0) == 0)
    def _():
        sum_ref[...] = jnp.zeros_like(sum_ref)

    up = piece_rows(up_ref)
    down = piece_rows(down_ref)
    for r in range(x_ref.shape[0] // RB):
        rows = slice(r * RB, (r + 1) * RB)
        hidden = mm(x_ref[rows, :], up) + bias_ref[0]
        area = 0.5 * (1.0 + lax.erf(hidden * (2.0**-0.5)))
        activated = (hidden * area).astype(BF)
        act_ref[rows, :] = activated
        slope_ref[rows, :] = (area + hidden * jnp.exp(-0.5 * hidden * hidden) * ((2.0 * jnp.pi) ** -0.5)).astype(BF)
        sum_ref[rows, :] += mm_nt(activated, down)


def feed_forward(x, weights, bias):
    length, features = x.shape
    dp, parts, cut, _ = weights.shape
    units = bias.shape[-1]
    piece = (dp, 1, cut, units)
    return pl.pallas_call(
        feed_forward_kernel,
        name="feed_forward",
        out_shape=(
            jax.ShapeDtypeStruct((length, parts * units), BF),
            jax.ShapeDtypeStruct((length, parts * units), BF),
            jax.ShapeDtypeStruct((length, features), F32),
        ),
        grid=(parts,),
        in_specs=[
            pl.BlockSpec((length, features), lambda t: (0, 0)),
            pl.BlockSpec(piece, lambda t: (0, t, 0, 0)),
            pl.BlockSpec(piece, lambda t: (0, t, 0, 1)),
            pl.BlockSpec((1, 1, units), lambda t: (t, 0, 0)),
        ],
        out_specs=(
            pl.BlockSpec((length, units), lambda t: (0, t)),
            pl.BlockSpec((length, units), lambda t: (0, t)),
            pl.BlockSpec((length, features), lambda t: (0, 0)),
        ),
        cost_estimate=pl.CostEstimate(
            flops=4 * length * features * parts * units,
            transcendentals=2 * length * parts * units,
            bytes_accessed=length * (parts * units * 4 + features * 6),
        ),
        compiler_params=pltpu.CompilerParams(dimension_semantics=("arbitrary",)),
    )(x, weights, weights, bias)


def feed_forward_backward_kernel(
    grad_ref, x_ref, act_ref, slope_ref, up_ref, down_ref, pack_ref, back_ref, bias_ref, xt_ref, gt_ref, gh_ref
):
    @pl.when(pl.program_id(0) == 0)
    def _():
        back_ref[...] = jnp.zeros_like(back_ref)
        xt_ref[...] = x_ref[...].T
        gt_ref[...] = grad_ref[...].T

    up = piece_rows(up_ref)
    down = piece_rows(down_ref)
    total = jnp.zeros((1, act_ref.shape[1]), F32)
    for r in range(x_ref.shape[0] // RB):
        rows = slice(r * RB, (r + 1) * RB)
        grad_hidden = (mm(grad_ref[rows, :], down) * slope_ref[rows, :].astype(F32)).astype(BF)
        gh_ref[rows, :] = grad_hidden
        total = total + jnp.sum(grad_hidden.astype(F32), axis=0, keepdims=True)
        back_ref[rows, :] += mm_nt(grad_hidden, up)
    bias_ref[0] = total
    units = act_ref.shape[1]
    split = (pack_ref.shape[0], pack_ref.shape[2], units)
    pack_ref[:, 0, :, 0:units] = mm(xt_ref[...], gh_ref[...]).astype(BF).reshape(split)
    pack_ref[:, 0, :, units : 2 * units] = mm(gt_ref[...], act_ref[...]).astype(BF).reshape(split)


def feed_forward_backward(grad, x, act, slope, weights):
    length, features = x.shape
    dp, parts, cut, width = weights.shape
    units = act.shape[1] // parts
    piece = (dp, 1, cut, units)
    whole = pl.BlockSpec((length, features), lambda t: (0, 0))
    part = pl.BlockSpec((length, units), lambda t: (0, t))
    return pl.pallas_call(
        feed_forward_backward_kernel,
        name="feed_forward_backward",
        out_shape=(
            jax.ShapeDtypeStruct((dp, parts, cut, width), BF),
            jax.ShapeDtypeStruct((length, features), F32),
            jax.ShapeDtypeStruct((parts, 1, units), F32),
        ),
        grid=(parts,),
        in_specs=[
            whole,
            whole,
            part,
            part,
            pl.BlockSpec(piece, lambda t: (0, t, 0, 0)),
            pl.BlockSpec(piece, lambda t: (0, t, 0, 1)),
        ],
        out_specs=(
            pl.BlockSpec((dp, 1, cut, 2 * units), lambda t: (0, t, 0, 0)),
            whole,
            pl.BlockSpec((1, 1, units), lambda t: (t, 0, 0)),
        ),
        scratch_shapes=[
            pltpu.VMEM((features, length), BF),
            pltpu.VMEM((features, length), BF),
            pltpu.VMEM((length, units), BF),
        ],
        cost_estimate=pl.CostEstimate(
            flops=8 * length * features * parts * units,
            transcendentals=0,
            bytes_accessed=length * (parts * units * 4 + features * 8) + dp * parts * cut * width * 4,
        ),
        compiler_params=pltpu.CompilerParams(dimension_semantics=("arbitrary",)),
    )(grad, x, act, slope, weights, weights)


def output_gradient_kernel(grad_ref, context_ref, _, pack_ref, full_ref):
    part = pl.program_id(0)
    columns = context_ref.shape[1] // 4

    @pl.when(part == 0)
    def _():
        full_ref[...] = mm(grad_ref[...].T, context_ref[...])

    split = (pack_ref.shape[0], pack_ref.shape[2], pack_ref.shape[3])
    for t in range(4):

        @pl.when(part == t)
        def _():
            at = (t % 2 * 2 + t // 2) * columns
            piece = full_ref[:, at : at + columns]
            rest = jnp.zeros((piece.shape[0], split[2] - columns), F32)
            pack_ref[:, 0] = jnp.concatenate([piece, rest], axis=1).astype(BF).reshape(split)


def output_gradient(grad, context, pack):
    length, features = grad.shape
    dp, parts, cut, width = pack.shape
    whole = pl.BlockSpec((length, features), lambda t: (0, 0))
    return pl.pallas_call(
        output_gradient_kernel,
        name="output_gradient",
        out_shape=jax.ShapeDtypeStruct(pack.shape, BF),
        grid=(parts,),
        in_specs=[whole, whole, pl.BlockSpec(memory_space=pl.ANY)],
        out_specs=pl.BlockSpec((dp, 1, cut, PAIR * 2), lambda t: (0, t, 0, width // (PAIR * 2) - 1)),
        scratch_shapes=[pltpu.VMEM((features, features), F32)],
        input_output_aliases={2: 0},
        cost_estimate=pl.CostEstimate(
            flops=2 * length * features * features, transcendentals=0, bytes_accessed=length * features * 4
        ),
        compiler_params=pltpu.CompilerParams(dimension_semantics=("arbitrary",)),
    )(grad, context, pack)


def small_turns(bits):
    return [0, bits] + list(reversed(range(1, bits)))


def tiny_turns(bits):
    return list(range(1, bits)) + [0, bits]


def make_per_device(dp):
    bits = dp.bit_length() - 1
    assert dp == 1 << bits

    def per_device(
        tokens,
        segment_ids,
        w_query,
        w_key,
        w_value,
        w_out,
        b_query,
        b_value,
        w_up,
        w_down,
        b_up,
        b_out,
        gain_one,
        shift_one,
        b_down,
        gain_two,
        shift_two,
        cotangent,
    ):
        place = lax.axis_index("tensor")
        depth = lax.axis_index("dp")
        across = place // 2
        core = place % 2
        _, quarter, features = tokens.shape
        cut, columns = w_query.shape
        units = w_up.shape[1]
        half = 2 * columns
        pairs = half // PAIR
        first_core = core == 0
        first_chip = across == 0
        tiled = cut % 16 == 0
        groups = (dp, cut) if tiled else (1, dp * cut)

        def swap_chips(value):
            return lax.ppermute(value, "tensor", [(0, 2), (2, 0), (1, 3), (3, 1)])

        def swap_cores(value):
            return lax.ppermute(value, "tensor", [(0, 1), (1, 0), (2, 3), (3, 2)])

        def swap_bit(value, b):
            return lax.ppermute(value, "dp", [(i, i ^ (1 << b)) for i in range(dp)])

        def bit_of(b):
            return (depth >> b) & 1

        def in_order(flag, mine, other, axis):
            return jnp.stack([jnp.where(flag, mine, other), jnp.where(flag, other, mine)], axis=axis)

        def mine_of(value, index, axis):
            return lax.dynamic_index_in_dim(value, index, axis, keepdims=False)

        attention_pack = jnp.concatenate([w_query, w_key, w_value], axis=1)
        if tiled:
            gathered = jnp.stack([attention_pack, swap_chips(attention_pack)])
            for b in reversed(range(bits)):
                before_last = gathered
                gathered = jnp.concatenate([gathered, swap_bit(gathered, b)])
            spot = jnp.stack([depth, across]).astype(jnp.int32)
        else:
            gathered = lax.all_gather(attention_pack, BOTH, axis=0).reshape(dp, 2, 2, cut, 3 * columns)
            gathered = mine_of(gathered, core, 2).transpose(1, 0, 2, 3).reshape(2, dp * cut, 3 * columns)
            spot = jnp.zeros((2,), jnp.int32)

        tokens_own = in_order(first_chip, mine_of(tokens, across, 0), swap_chips(mine_of(tokens, 1 - across, 0)), 0)
        tokens_full = in_order(first_core, tokens_own, swap_cores(tokens_own), 1).reshape(4 * quarter, features)
        tokens_own = tokens_own.reshape(2 * quarter, features)

        small = [b_query, b_value, b_up, b_out, gain_one, shift_one, b_down, gain_two, shift_two]
        sizes = [v.size for v in small]
        lanes = -(-sum(sizes) // PAIR) * PAIR
        packed = jnp.concatenate([v.reshape(-1) for v in small])
        small_all = jnp.pad(packed, (0, lanes - packed.size)).reshape(1, lanes)
        turns = small_turns(bits)
        for b in turns:
            if b == bits:
                small_all = in_order(first_chip, small_all, swap_chips(small_all), 0)
            else:
                small_all = in_order(bit_of(b) == 0, small_all, swap_bit(small_all, b), 0)
        axes = turns[::-1]
        where = [axes.index(b) for b in reversed(range(bits))] + [axes.index(bits)]
        small_all = small_all.transpose(*where, bits + 1, bits + 2).reshape(dp, 2, 1, lanes)
        core_bias = small_all[:, :, 0, : sizes[0] + sizes[1]].reshape(dp, 2, 2, *b_query.shape).astype(F32)
        core_bias = core_bias.transpose(2, 1, 3, 0, 4).reshape(2, pairs, PAIR)
        bias_mine = jnp.stack([core_bias[0], jnp.zeros((pairs, PAIR), F32), core_bias[1]], axis=1).reshape(1, 3 * half)
        small_all = in_order(first_core, small_all, swap_cores(small_all), 2).reshape(dp, 4, lanes)
        pieces = []
        offset = 0
        for v, size in zip(small, sizes):
            piece = small_all[:, :, offset : offset + size].astype(F32)
            offset += size
            if v.ndim == 2:
                pieces.append(piece.reshape(dp, 4, *v.shape).transpose(1, 2, 0, 3))
            else:
                pieces.append(piece.reshape(-1))
        _, _, bias_up, out_bias, gain1, shift1, down_bias, gain2, shift2 = pieces
        bias_up = bias_up.reshape(4, 1, units)

        spare = jnp.zeros((cut, 2 * PAIR - columns), BF)
        other_pack = jnp.concatenate([w_up, w_down.T, w_out.T, spare], axis=1)
        width = other_pack.shape[1]
        if tiled:
            other_pack, _ = lax.optimization_barrier((other_pack, before_last))
        others = lax.all_gather(other_pack, BOTH, axis=0).reshape(dp, 4, cut, width)
        if not tiled:
            others = others.transpose(1, 0, 2, 3).reshape(1, 4, dp * cut, width)

        cotangent_sent = mine_of(cotangent, 1 - across, 0).astype(BF)
        cotangent_own = in_order(
            first_chip,
            mine_of(cotangent, across, 0),
            swap_chips(cotangent_sent).astype(F32),
            0,
        ).reshape(2 * quarter, features)
        segments = segment_bounds(mine_of(segment_ids, across, 0))

        *operands, w_qkv, limits = project(tokens_full, gathered, bias_mine, spot, *segments[3:])
        heads_out, lse = attention_forward(operands, limits, segments)

        by_core = heads_out.reshape(2, 2, quarter, half)
        kept = mine_of(by_core, core, 1)
        got = swap_cores(mine_of(by_core, 1 - core, 1))
        context = in_order(first_core, kept, got, 2).reshape(2 * quarter, 2 * half)

        w_out_t = (
            others[..., 2 * units : 2 * units + columns]
            .reshape(groups[0], 2, 2, groups[1], columns)
            .transpose(0, 3, 2, 1, 4)
            .reshape(features, features)
        )
        summed = tokens_own.astype(F32) + mm_nt(context, w_out_t) + out_bias
        hat1, inverse1 = statistics(summed)
        normed = hat1 * gain1 + shift1
        normed_low = normed.astype(BF)
        activated, slope, branch = feed_forward(normed_low, others, bias_up)
        hat2, inverse2 = statistics(normed + branch + down_bias)
        out_own = (hat2 * gain2 + shift2).reshape(2, quarter, features)

        def send_back(value):
            kept_part = mine_of(value, across, 0)
            got_part = swap_chips(mine_of(value, 1 - across, 0).astype(BF)).astype(F32)
            return in_order(first_chip, kept_part, got_part, 0)

        layer_out = send_back(out_own)

        grad_z = norm_backward(cotangent_own, hat2, inverse2, gain2)
        grad_branch = grad_z.astype(BF)
        pack, back, grad_bias_up = feed_forward_backward(grad_branch, normed_low, activated, slope, others)
        grad_normed = grad_z + back
        grad_summed = norm_backward(grad_normed, hat1, inverse1, gain1)
        grad_attended = grad_summed.astype(BF)
        pack = output_gradient(grad_attended, context, pack)
        if not tiled:
            pack = pack.reshape(4, dp, cut, width).transpose(1, 0, 2, 3)
        others_mine = lax.psum_scatter(pack.reshape(4 * dp, cut, width), BOTH, scatter_dimension=0, tiled=False)

        grad_context = mm(grad_attended, w_out_t).astype(BF).reshape(2, quarter, 2, half)
        kept = mine_of(grad_context, core, 2)
        got = swap_cores(mine_of(grad_context, 1 - core, 2))
        grad_heads = in_order(first_core, kept, got, 1).reshape(4 * quarter, half)

        grad_qkv = attention_backward(operands, grad_heads, heads_out, lse, limits, segments)
        part = mm_nt(grad_qkv, w_qkv).reshape(2, 2, quarter, features)
        part_kept = mine_of(part, core, 1)
        part_got = swap_cores(mine_of(part, 1 - core, 1).astype(BF))
        grad_tokens = send_back(grad_summed.reshape(2, quarter, features) + part_kept + part_got.astype(F32))

        def halve(value, flag, swap, axis, kind):
            kept_half = mine_of(value, flag, axis)
            sent_half = mine_of(value, 1 - flag, axis)
            return (kept_half.astype(F32) + swap(sent_half).astype(F32)).astype(kind)

        grad_w = mm_tn(tokens_full, grad_qkv).astype(BF).reshape(dp, cut, 3 * half)
        for b in range(bits):
            grad_w = halve(grad_w.reshape(-1, 2, cut, 3 * half), bit_of(b), lambda v: swap_bit(v, b), 1, BF)
        grad_w = (
            grad_w.reshape(cut, pairs, 3, PAIR).transpose(0, 2, 1, 3).reshape(cut, 3, 2, columns).transpose(2, 0, 1, 3)
        )
        grad_w = halve(grad_w.reshape(2, cut, 3 * columns), across, lambda v: swap_chips(v), 0, F32)

        bias_grads = jnp.sum(grad_qkv.astype(F32), axis=0).reshape(pairs, 3, PAIR)

        def matrix_small(value, like):
            return value.reshape(2, 2, like.shape[0], dp, like.shape[1]).transpose(3, 0, 1, 2, 4).reshape(dp, 2, 2, -1)

        def head_small(value, like):
            value = value.reshape(2, columns)
            zero = jnp.zeros_like(value)
            both = [jnp.where(first_core, value, zero), jnp.where(first_core, zero, value)]
            return matrix_small(jnp.stack(both, axis=1), like)

        def vector_small(value):
            return value.reshape(dp, 2, 2, -1)

        small_grads = jnp.concatenate(
            [
                head_small(bias_grads[:, 0], b_query),
                head_small(bias_grads[:, 2], b_value),
                matrix_small(grad_bias_up, b_up),
                vector_small(jnp.sum(grad_summed, axis=0)),
                vector_small(jnp.sum(grad_normed * hat1, axis=0)),
                vector_small(jnp.sum(grad_normed, axis=0)),
                vector_small(jnp.sum(grad_z, axis=0)),
                vector_small(jnp.sum(cotangent_own * hat2, axis=0)),
                vector_small(jnp.sum(cotangent_own, axis=0)),
            ],
            axis=3,
        )
        small_grads = jnp.pad(small_grads, ((0, 0), (0, 0), (0, 0), (0, lanes - small_grads.shape[3])))
        small_grads = halve(small_grads, core, lambda v: swap_cores(v), 2, F32)
        small_grads = small_grads.reshape((2,) * (bits + 1) + (lanes,))
        left = list(reversed(range(bits))) + [bits]
        for b in tiny_turns(bits):
            if b == bits:
                small_grads = halve(small_grads, across, lambda v: swap_chips(v), left.index(b), F32)
            else:
                small_grads = halve(small_grads, bit_of(b), lambda v: swap_bit(v, b), left.index(b), F32)
            left.remove(b)

        others_mine = others_mine.astype(F32)
        small_out = []
        offset = 0
        for v, size in zip(small, sizes):
            small_out.append(small_grads[offset : offset + size].reshape(v.shape))
            offset += size
        return (
            layer_out,
            grad_tokens,
            grad_w[:, :columns],
            grad_w[:, columns : 2 * columns],
            grad_w[:, 2 * columns :],
            others_mine[:, 2 * units : 2 * units + columns].T,
            small_out[0],
            small_out[1],
            others_mine[:, :units],
            others_mine[:, units : 2 * units].T,
            small_out[2],
            small_out[3],
            small_out[4],
            small_out[5],
            small_out[6],
            small_out[7],
            small_out[8],
        )

    return per_device


def solution(mesh):
    rows = P("dp", "tensor", None)
    split = P("dp", "tensor")
    turned = P("tensor", "dp")
    vector = P(("dp", "tensor"))
    in_specs = (rows, P("dp", None), split, split, split, turned, turned, turned, split, turned, turned)
    in_specs += (vector,) * 6 + (rows,)
    out_specs = (rows, rows, split, split, split, turned, turned, turned, split, turned, turned)
    out_specs += (vector,) * 6
    dp = mesh.shape["dp"]
    inner = make_per_device(dp)

    return jax.shard_map(inner, mesh=mesh, in_specs=in_specs, out_specs=out_specs, check_vma=False)
```

```python
import jax
import jax.numpy as jnp
from jax import lax
from jax.experimental import pallas as pl
from jax.experimental.pallas import tpu as pltpu
from jax.sharding import PartitionSpec as P


HD = 64
PAIR = 2 * HD
SEGS = 12
QB = 512
KB = 256
RB = 256
NEG = -1e30
LIMIT = 50.0
GAP = 256.0
FREE = SEGS + 1
EPS = 1e-12
BF = jnp.bfloat16
F32 = jnp.float32
BOTH = ("dp", "tensor")
NT = (((1,), (1,)), ((), ()))


def own_lanes(shape, h):
    lane = lax.broadcasted_iota(jnp.int32, shape, 1)
    return (lane < HD) if h % 2 == 0 else (lane >= HD)


def with_column(base, column, h):
    lane = lax.broadcasted_iota(jnp.int32, base.shape, 1) - (HD if h % 2 == 0 else 0)
    high = column.astype(BF).astype(F32)
    middle = (column - high).astype(BF).astype(F32)
    low = column - high - middle
    base = jnp.where(lane == FREE, high, base)
    base = jnp.where(lane == FREE + 1, middle, base)
    return jnp.where(lane == FREE + 2, low, base)


def fits(limit_ref, heads):
    largest = limit_ref[0, 0] * limit_ref[0, heads]
    for h in range(1, heads):
        largest = jnp.maximum(largest, limit_ref[0, h] * limit_ref[0, heads + h])
    return largest <= LIMIT * LIMIT


def attention_forward_kernel(
    lo_ref, hi_ref, spot_ref, limit_ref, bound_ref, q_ref, key_ref, val_ref, kept_ref, sent_ref, lse_ref, acc_ref, top_ref
):
    row = pl.program_id(0)
    heads = key_ref.shape[1] // PAIR
    acc_ref[...] = jnp.zeros_like(acc_ref)
    plain = fits(limit_ref, heads)

    @pl.when(plain)
    def _():
        def step(kb, carry):
            there = pl.ds(pl.multiple_of(kb * KB, KB), KB)
            for h in range(heads):
                cols = slice(h * PAIR, (h + 1) * PAIR)
                scores = lax.dot_general(q_ref[:, cols], key_ref[there, cols], NT, preferred_element_type=F32)
                raised = jnp.exp(scores).astype(BF)
                acc_ref[:, cols] += jnp.dot(raised, val_ref[there, cols], preferred_element_type=F32)
            return carry

        lax.fori_loop(lo_ref[row], hi_ref[row], step, 0)
        top_ref[...] = jnp.zeros_like(top_ref)

    @pl.when(jnp.logical_not(plain))
    def _():
        start = bound_ref[0, 0:1, :].T
        end = bound_ref[0, 1:2, :].T
        top_ref[...] = jnp.full_like(top_ref, NEG)

        def step(kb, carry):
            base = pl.multiple_of(kb * KB, KB)
            there = pl.ds(base, KB)
            place = base + lax.broadcasted_iota(jnp.int32, (QB, KB), 1)
            valid = (place >= start) & (place < end)
            for h in range(heads):
                cols = slice(h * PAIR, (h + 1) * PAIR)
                scores = lax.dot_general(q_ref[:, cols], key_ref[there, cols], NT, preferred_element_type=F32)
                scores = jnp.where(valid, scores, NEG)
                before = top_ref[:, h : h + 1]
                top = jnp.maximum(before, jnp.max(scores, axis=1, keepdims=True))
                raised = jnp.exp(scores - top).astype(BF)
                acc_ref[:, cols] = jnp.exp(before - top) * acc_ref[:, cols] + jnp.dot(
                    raised, val_ref[there, cols], preferred_element_type=F32
                )
                top_ref[:, h : h + 1] = top
            return carry

        lax.fori_loop(lo_ref[row], hi_ref[row], step, 0)

    lse = top_ref[...]
    outs = []
    lane = lax.broadcasted_iota(jnp.int32, (QB, PAIR), 1)
    for p in range(heads // 2):
        both = []
        for h in (2 * p, 2 * p + 1):
            block = acc_ref[:, h * PAIR : (h + 1) * PAIR]
            at = SEGS + (HD if h % 2 == 0 else 0)
            total = block[:, at : at + 1]
            both.append(block / total)
            lse = jnp.where(lane == h, lse + jnp.log(total), lse)
        outs.append(jnp.where(lane < HD, both[0], both[1]).astype(BF))
    lse_ref[...] = lse

    def put(ref):
        for p in range(heads // 2):
            ref[0, :, p * PAIR : (p + 1) * PAIR] = outs[p]

    stays = row % 2 == spot_ref[1]
    pl.when(stays)(lambda: put(kept_ref))
    pl.when(jnp.logical_not(stays))(lambda: put(sent_ref))


def attention_backward_kernel(
    lo_ref,
    hi_ref,
    spot_ref,
    limit_ref,
    bound_ref,
    lse_ref,
    q_ref,
    key_ref,
    val_ref,
    kt_ref,
    grad_kept_ref,
    grad_got_ref,
    kept_ref,
    sent_ref,
    out_ref,
    dq_ref,
    dk_ref,
    dv_ref,
):
    row = pl.program_id(0)
    heads = key_ref.shape[1] // PAIR
    pairs = heads // 2

    @pl.when(row == 0)
    def _():
        dk_ref[...] = jnp.zeros_like(dk_ref)
        dv_ref[...] = jnp.zeros_like(dv_ref)

    here = pl.ds(pl.multiple_of(row * QB, QB), QB)
    stays = row % 2 == spot_ref[1]
    q_parts, g_parts, q_score, g_score = [], [], [], []
    for p in range(pairs):
        cols = slice(p * PAIR, (p + 1) * PAIR)
        grad = jnp.where(stays, grad_kept_ref[0, :, cols].astype(F32), grad_got_ref[0, :, cols].astype(F32))
        product = grad * jnp.where(stays, kept_ref[0, :, cols].astype(F32), sent_ref[0, :, cols].astype(F32))
        for h in (2 * p, 2 * p + 1):
            block = q_ref[:, h * PAIR : (h + 1) * PAIR].astype(F32)
            own = own_lanes(block.shape, h)
            inner = jnp.sum(jnp.where(own, product, 0.0), axis=1, keepdims=True)
            g_own = jnp.where(own, grad, 0.0)
            q_parts.append(jnp.where(own, block, 0.0).astype(BF))
            g_parts.append(g_own.astype(BF))
            q_score.append(with_column(block, -lse_ref[:, h : h + 1], h).astype(BF))
            g_score.append(with_column(g_own, -inner, h).astype(BF))
    dq_ref[...] = jnp.zeros_like(dq_ref)

    def sweep(masked):
        start = bound_ref[0, 0:1, :]
        end = bound_ref[0, 1:2, :]

        def step(kb, carry):
            base = pl.multiple_of(kb * KB, KB)
            there = pl.ds(base, KB)
            if masked:
                place = base + lax.broadcasted_iota(jnp.int32, (KB, QB), 0)
                valid = (place >= start) & (place < end)
            for p in range(pairs):
                cols = slice(p * PAIR, (p + 1) * PAIR)
                dk = dk_ref[there, cols]
                dv = dv_ref[there, cols]
                for h in (2 * p, 2 * p + 1):
                    keys = key_ref[there, h * PAIR : (h + 1) * PAIR]
                    vals = val_ref[there, h * PAIR : (h + 1) * PAIR]
                    scores = lax.dot_general(keys, q_score[h], NT, preferred_element_type=F32)
                    if masked:
                        scores = jnp.where(valid, scores, NEG)
                    weights = jnp.exp(scores)
                    grad_scores = weights * lax.dot_general(vals, g_score[h], NT, preferred_element_type=F32)
                    grad_scores = grad_scores.astype(BF)
                    dv = dv + jnp.dot(weights.astype(BF), g_parts[h], preferred_element_type=F32)
                    dk = dk + jnp.dot(grad_scores, q_parts[h], preferred_element_type=F32)
                    rows = slice(h * HD, (h + 1) * HD)
                    dq_ref[rows, :] += jnp.dot(kt_ref[rows, there], grad_scores, preferred_element_type=F32)
                dk_ref[there, cols] = dk
                dv_ref[there, cols] = dv
            return carry

        lax.fori_loop(lo_ref[row], hi_ref[row], step, 0)

    plain = fits(limit_ref, heads)
    pl.when(plain)(lambda: sweep(False))
    pl.when(jnp.logical_not(plain))(lambda: sweep(True))
    for p in range(pairs):
        cols = slice(p * PAIR, (p + 1) * PAIR)
        out_ref[here, 3 * p * PAIR : (3 * p + 1) * PAIR] = (dq_ref[cols, :] * HD ** (-0.5)).T.astype(BF)

    @pl.when(row == pl.num_programs(0) - 1)
    def _():
        for p in range(pairs):
            cols = slice(p * PAIR, (p + 1) * PAIR)
            out_ref[:, (3 * p + 1) * PAIR : (3 * p + 2) * PAIR] = dk_ref[:, cols].astype(BF)
            out_ref[:, (3 * p + 2) * PAIR : (3 * p + 3) * PAIR] = dv_ref[:, cols].astype(BF)


def attention_forward(operands, limits, segments, spot):
    queries, keys, values, _ = operands
    lo, hi, bounds = segments[:3]
    length, wide = keys.shape
    heads = wide // PAIR
    assert length == 4 * QB
    whole = pl.BlockSpec((length, wide), lambda i, *_: (0, 0))
    return pl.pallas_call(
        attention_forward_kernel,
        name="attention_forward",
        out_shape=(
            jax.ShapeDtypeStruct((2, QB, heads * HD), BF),
            jax.ShapeDtypeStruct((2, QB, heads * HD), BF),
            jax.ShapeDtypeStruct((length, PAIR), F32),
        ),
        grid_spec=pltpu.PrefetchScalarGridSpec(
            num_scalar_prefetch=3,
            grid=(4,),
            in_specs=[
                pl.BlockSpec(memory_space=pltpu.SMEM),
                pl.BlockSpec((1, 2, QB), lambda i, *_: (i, 0, 0)),
                pl.BlockSpec((QB, wide), lambda i, *_: (i, 0)),
                whole,
                whole,
            ],
            out_specs=(
                pl.BlockSpec((1, QB, heads * HD), lambda i, *_: (i // 2, 0, 0)),
                pl.BlockSpec((1, QB, heads * HD), lambda i, *_: (i // 2, 0, 0)),
                pl.BlockSpec((QB, PAIR), lambda i, *_: (i, 0)),
            ),
            scratch_shapes=[pltpu.VMEM((QB, wide), F32), pltpu.VMEM((QB, PAIR), F32)],
        ),
        cost_estimate=pl.CostEstimate(
            flops=length * length * wide * 2,
            transcendentals=length * length * heads,
            bytes_accessed=keys.size * 7,
        ),
        compiler_params=pltpu.CompilerParams(dimension_semantics=("arbitrary",)),
    )(lo, hi, spot, limits, bounds, queries, keys, values)


def attention_backward(operands, grads, outs, lse, limits, segments, spot):
    queries, keys, values, turned = operands
    lo, hi, bounds = segments[:3]
    length, wide = keys.shape
    heads = wide // PAIR
    width = heads * HD
    assert length == 4 * QB
    whole = pl.BlockSpec((length, wide), lambda i, *_: (0, 0))
    rows = pl.BlockSpec((1, QB, width), lambda i, *_: (i // 2, 0, 0))
    return pl.pallas_call(
        attention_backward_kernel,
        name="attention_backward",
        out_shape=jax.ShapeDtypeStruct((length, 3 * width), BF),
        grid_spec=pltpu.PrefetchScalarGridSpec(
            num_scalar_prefetch=3,
            grid=(4,),
            in_specs=[
                pl.BlockSpec(memory_space=pltpu.SMEM),
                pl.BlockSpec((1, 2, QB), lambda i, *_: (i, 0, 0)),
                pl.BlockSpec((QB, PAIR), lambda i, *_: (i, 0)),
                pl.BlockSpec((QB, wide), lambda i, *_: (i, 0)),
                whole,
                whole,
                pl.BlockSpec((width, length), lambda i, *_: (0, 0)),
                rows,
                rows,
                rows,
                rows,
            ],
            out_specs=pl.BlockSpec((length, 3 * width), lambda i, *_: (0, 0)),
            scratch_shapes=[
                pltpu.VMEM((width, QB), F32),
                pltpu.VMEM((length, width), F32),
                pltpu.VMEM((length, width), F32),
            ],
        ),
        cost_estimate=pl.CostEstimate(
            flops=length * length * wide * 5,
            transcendentals=length * length * heads,
            bytes_accessed=keys.size * 11,
        ),
        compiler_params=pltpu.CompilerParams(dimension_semantics=("arbitrary",)),
    )(lo, hi, spot, limits, bounds, lse, queries, keys, values, turned, *grads, *outs)


def segment_bounds(segments):
    length = segments.shape[0]
    names = jnp.arange(SEGS, dtype=jnp.int32)[:, None]
    counts = jnp.sum((segments[None, :] == names).astype(jnp.int32), axis=1, keepdims=True)
    start = jnp.sum(jnp.where(segments[None, :] > names, counts, 0), axis=0)
    end = jnp.sum(jnp.where(segments[None, :] >= names, counts, 0), axis=0)
    start = start.reshape(length // QB, QB)
    end = end.reshape(length // QB, QB)
    lo = start[:, 0] // KB
    hi = (end[:, -1] + (KB - 1)) // KB
    lane = jnp.arange(PAIR, dtype=jnp.int32)[None, :] % HD
    same = lane == segments[:, None]
    pattern = jnp.where((lane < SEGS) & same | (lane >= SEGS) & (lane < FREE + 3), 1.0, 0.0).astype(BF)
    qpattern = jnp.where(lane == SEGS, -GAP, jnp.where(same, GAP, 0.0)).astype(BF)
    return lo, hi, jnp.stack([start, end], axis=1), pattern, qpattern


def statistics(rows):
    centred = rows - jnp.mean(rows, axis=-1, keepdims=True)
    inverse = lax.rsqrt(jnp.mean(centred * centred, axis=-1, keepdims=True) + EPS)
    return centred * inverse, inverse


def norm_backward(grad, hat, inverse, gain):
    scaled = grad * gain
    return inverse * (
        scaled
        - jnp.mean(scaled, axis=-1, keepdims=True)
        - hat * jnp.mean(scaled * hat, axis=-1, keepdims=True)
    )


def mm(a, b):
    return lax.dot_general(a, b, (((1,), (0,)), ((), ())), preferred_element_type=F32)


def mm_nt(a, b):
    return lax.dot_general(a, b, NT, preferred_element_type=F32)


def mm_tn(a, b):
    return lax.dot_general(a, b, (((0,), (0,)), ((), ())), preferred_element_type=F32)


def piece_rows(ref):
    block = ref[:, 0]
    return block.reshape(block.shape[0] * block.shape[1], block.shape[2])


def project_kernel(
    spot_ref, tokens_ref, weights_ref, bias_ref, pattern_ref, qpattern_ref, q_ref, k_ref, v_ref, kt_ref, w_ref, limit_ref
):
    slots, cut, width = weights_ref.shape
    columns = width // 3
    bits = (slots // 2).bit_length() - 1
    pairs = 2 * columns // PAIR

    @pl.when(pl.program_id(0) == 0)
    def _():
        for d in range(slots // 2):
            other = d ^ spot_ref[0]
            slot = 0
            for b in range(bits):
                slot = slot * 2 + ((other >> b) & 1)
            first = weights_ref[slot * 2 + spot_ref[1]].astype(F32)
            second = weights_ref[slot * 2 + 1 - spot_ref[1]].astype(F32)
            for s in range(3):
                cols = slice(s * columns, (s + 1) * columns)
                joined = jnp.concatenate([first[:, cols], second[:, cols]], axis=1).astype(BF)
                for p in range(pairs):
                    at = (3 * p + s) * PAIR
                    w_ref[d * cut : (d + 1) * cut, at : at + PAIR] = joined[:, p * PAIR : (p + 1) * PAIR]
        limit_ref[...] = jnp.zeros_like(limit_ref)

    pattern = pattern_ref[...].astype(F32)
    qpattern = qpattern_ref[...].astype(F32)
    lane = lax.broadcasted_iota(jnp.int32, (8, PAIR), 1)[0:1, :]
    largest = limit_ref[...]
    for p in range(pairs):
        cols = slice(3 * p * PAIR, 3 * (p + 1) * PAIR)
        result = (mm(tokens_ref[...], w_ref[:, cols]) + bias_ref[:, cols]).astype(BF).astype(F32)
        queries = result[:, :PAIR] * HD ** (-0.5)
        keys = result[:, PAIR : 2 * PAIR]
        values = result[:, 2 * PAIR :]
        kt_ref[p * PAIR : (p + 1) * PAIR, :] = keys.astype(BF).T
        for h in (2 * p, 2 * p + 1):
            own = own_lanes(queries.shape, h)
            at = slice(h * PAIR, (h + 1) * PAIR)
            q_ref[:, at] = jnp.where(own, queries, qpattern).astype(BF)
            k_ref[:, at] = jnp.where(own, keys, pattern).astype(BF)
            v_ref[:, at] = jnp.where(own, values, pattern).astype(BF)
            for kind, part in enumerate((queries, keys)):
                square = jnp.sum(jnp.where(own, part * part, 0.0), axis=1, keepdims=True)
                peak = jnp.max(square, axis=0, keepdims=True)
                largest = jnp.where(lane == kind * 2 * pairs + h, jnp.maximum(largest, peak), largest)
    limit_ref[...] = largest


def project(tokens, weights, bias, spot, pattern, qpattern):
    length, features = tokens.shape
    width = 2 * weights.shape[2]
    wide = 2 * width // 3
    lanes = pl.BlockSpec((RB, PAIR), lambda i, spot: (i, 0))
    rows = pl.BlockSpec((RB, wide), lambda i, spot: (i, 0))
    return pl.pallas_call(
        project_kernel,
        name="project",
        out_shape=(
            jax.ShapeDtypeStruct((length, wide), BF),
            jax.ShapeDtypeStruct((length, wide), BF),
            jax.ShapeDtypeStruct((length, wide), BF),
            jax.ShapeDtypeStruct((width // 3, length), BF),
            jax.ShapeDtypeStruct((features, width), BF),
            jax.ShapeDtypeStruct((1, PAIR), F32),
        ),
        grid_spec=pltpu.PrefetchScalarGridSpec(
            num_scalar_prefetch=1,
            grid=(length // RB,),
            in_specs=[
                pl.BlockSpec((RB, features), lambda i, spot: (i, 0)),
                pl.BlockSpec(weights.shape, lambda i, spot: (0, 0, 0)),
                pl.BlockSpec((1, width), lambda i, spot: (0, 0)),
                lanes,
                lanes,
            ],
            out_specs=(
                rows,
                rows,
                rows,
                pl.BlockSpec((width // 3, RB), lambda i, spot: (0, i)),
                pl.BlockSpec((features, width), lambda i, spot: (0, 0)),
                pl.BlockSpec((1, PAIR), lambda i, spot: (0, 0)),
            ),
        ),
        cost_estimate=pl.CostEstimate(
            flops=2 * length * features * width, transcendentals=0, bytes_accessed=2 * length * (features + 3 * wide)
        ),
        compiler_params=pltpu.CompilerParams(dimension_semantics=("arbitrary",)),
    )(spot, tokens, weights, bias, pattern, qpattern)


CHUNK = 128


def output_weights(piece_ref, spot_ref, w_ref):
    columns = w_ref.shape[2] // 2
    for k in range(2):
        core = spot_ref[1] if k == 0 else 1 - spot_ref[1]
        first = piece_ref[:, core].astype(F32)
        second = piece_ref[:, 2 + core].astype(F32)
        size = first.shape[0] * first.shape[1]
        joined = [x.reshape(size, x.shape[2])[:, :columns] for x in (first, second)]
        w_ref[k] = jnp.concatenate(joined, axis=1).astype(BF)


def feed_forward_kernel(
    spot_ref,
    kept_ref,
    got_ref,
    tokens_ref,
    cotangent_ref,
    vector_ref,
    out_w_ref,
    up_ref,
    down_ref,
    bias_ref,
    act_ref,
    slope_ref,
    hat_ref,
    inverse_ref,
    low_ref,
    keep_ref,
    send_ref,
    grad_ref,
    grad_low_ref,
    total_ref,
    sum_ref,
    w_ref,
):
    part = pl.program_id(0)
    length = low_ref.shape[0]
    out_bias, gain1, shift1, down_bias, gain2, shift2 = [vector_ref[i : i + 1, :] for i in range(6)]

    @pl.when(part == 0)
    def _():
        output_weights(out_w_ref, spot_ref, w_ref)
        sum_ref[...] = jnp.zeros_like(sum_ref)
        total_ref[...] = jnp.zeros_like(total_ref)

        def one(r, carry):
            rows = pl.ds(pl.multiple_of(r * CHUNK, CHUNK), CHUNK)
            attended = mm_nt(kept_ref[rows, :], w_ref[0]) + mm_nt(got_ref[rows, :], w_ref[1])
            hat, inverse = statistics(tokens_ref[rows, :].astype(F32) + attended + out_bias)
            hat_ref[rows, :] = hat
            inverse_ref[rows, :] = jnp.broadcast_to(inverse, (CHUNK, PAIR))
            low_ref[rows, :] = (hat * gain1 + shift1).astype(BF)
            return carry

        lax.fori_loop(0, length // CHUNK, one, 0)

    up = piece_rows(up_ref)
    down = piece_rows(down_ref)
    for r in range(length // RB):
        rows = slice(r * RB, (r + 1) * RB)
        hidden = mm(low_ref[rows, :], up) + bias_ref[0]
        area = 0.5 * (1.0 + lax.erf(hidden * (2.0**-0.5)))
        activated = (hidden * area).astype(BF)
        act_ref[rows, :] = activated
        slope_ref[rows, :] = (area + hidden * jnp.exp(-0.5 * hidden * hidden) * ((2.0 * jnp.pi) ** -0.5)).astype(BF)
        sum_ref[rows, :] += mm_nt(activated, down)

    @pl.when(part == pl.num_programs(0) - 1)
    def _():
        per_chip = keep_ref.shape[0] // CHUNK

        def one(r, carry):
            rows = pl.ds(pl.multiple_of(r * CHUNK, CHUNK), CHUNK)
            normed = hat_ref[rows, :] * gain1 + shift1
            hat, inverse = statistics(normed + sum_ref[rows, :] + down_bias)
            result = hat * gain2 + shift2
            stays = r // per_chip == spot_ref[0]
            there = pl.ds(pl.multiple_of(r % per_chip * CHUNK, CHUNK), CHUNK)

            @pl.when(stays)
            def _():
                keep_ref[there, :] = result

            @pl.when(jnp.logical_not(stays))
            def _():
                send_ref[there, :] = result.astype(BF)

            cotangent = cotangent_ref[rows, :]
            grad = norm_backward(cotangent, hat, inverse, gain2)
            grad_ref[rows, :] = grad
            grad_low_ref[rows, :] = grad.astype(BF)
            for i, value in enumerate((grad, cotangent * hat, cotangent)):
                total_ref[i : i + 1, :] += jnp.sum(value, axis=0, keepdims=True)
            return carry

        lax.fori_loop(0, length // CHUNK, one, 0)


def once(shape, zeros):
    return pl.BlockSpec(shape, lambda t, *_: zeros, pipeline_mode=pl.Buffered(1))


def feed_forward(spot, kept, got, tokens, cotangent, vectors, weights, bias):
    length, features = tokens.shape
    dp, parts, cut, width = weights.shape
    units = bias.shape[-1]
    half = kept.shape[1]
    piece = (dp, 1, cut, units)
    rows = pl.BlockSpec((length, features), lambda t, *_: (0, 0))
    chip = pl.BlockSpec((length // 2, features), lambda t, *_: (0, 0))
    part = pl.BlockSpec((length, units), lambda t, *_: (0, t))
    return pl.pallas_call(
        feed_forward_kernel,
        name="feed_forward",
        out_shape=(
            jax.ShapeDtypeStruct((length, parts * units), BF),
            jax.ShapeDtypeStruct((length, parts * units), BF),
            jax.ShapeDtypeStruct((length, features), F32),
            jax.ShapeDtypeStruct((length, PAIR), F32),
            jax.ShapeDtypeStruct((length, features), BF),
            jax.ShapeDtypeStruct((length // 2, features), F32),
            jax.ShapeDtypeStruct((length // 2, features), BF),
            jax.ShapeDtypeStruct((length, features), F32),
            jax.ShapeDtypeStruct((length, features), BF),
            jax.ShapeDtypeStruct((8, features), F32),
        ),
        grid_spec=pltpu.PrefetchScalarGridSpec(
            num_scalar_prefetch=1,
            grid=(parts,),
            in_specs=[
                once((length, half), (0, 0)),
                once((length, half), (0, 0)),
                once((length, features), (0, 0)),
                once((length, features), (0, 0)),
                once((8, features), (0, 0)),
                once((dp, parts, cut, 2 * PAIR), (0, 0, 0, width // (2 * PAIR) - 1)),
                pl.BlockSpec(piece, lambda t, *_: (0, t, 0, 0)),
                pl.BlockSpec(piece, lambda t, *_: (0, t, 0, 1)),
                pl.BlockSpec((1, 1, units), lambda t, *_: (t, 0, 0)),
            ],
            out_specs=(
                part,
                part,
                rows,
                pl.BlockSpec((length, PAIR), lambda t, *_: (0, 0)),
                rows,
                chip,
                chip,
                rows,
                rows,
                pl.BlockSpec((8, features), lambda t, *_: (0, 0)),
            ),
            scratch_shapes=[pltpu.VMEM((length, features), F32), pltpu.VMEM((2, features, half), BF)],
        ),
        cost_estimate=pl.CostEstimate(
            flops=4 * length * features * parts * units,
            transcendentals=2 * length * parts * units,
            bytes_accessed=length * (parts * units * 4 + features * 24),
        ),
        compiler_params=pltpu.CompilerParams(dimension_semantics=("arbitrary",)),
    )(spot, kept, got, tokens, cotangent, vectors, weights, weights, weights, bias)


def feed_forward_backward_kernel(
    grad_ref,
    x_ref,
    act_ref,
    slope_ref,
    up_ref,
    down_ref,
    direct_ref,
    hat_ref,
    inverse_ref,
    vector_ref,
    pack_ref,
    bias_ref,
    summed_ref,
    summed_low_ref,
    total_ref,
    back_ref,
    xt_ref,
    gt_ref,
    gh_ref,
):
    @pl.when(pl.program_id(0) == 0)
    def _():
        back_ref[...] = jnp.zeros_like(back_ref)
        total_ref[...] = jnp.zeros_like(total_ref)
        xt_ref[...] = x_ref[...].T
        gt_ref[...] = grad_ref[...].T

    up = piece_rows(up_ref)
    down = piece_rows(down_ref)
    total = jnp.zeros((1, act_ref.shape[1]), F32)
    for r in range(x_ref.shape[0] // RB):
        rows = slice(r * RB, (r + 1) * RB)
        grad_hidden = (mm(grad_ref[rows, :], down) * slope_ref[rows, :].astype(F32)).astype(BF)
        gh_ref[rows, :] = grad_hidden
        total = total + jnp.sum(grad_hidden.astype(F32), axis=0, keepdims=True)
        back_ref[rows, :] += mm_nt(grad_hidden, up)
    bias_ref[0] = total
    units = act_ref.shape[1]
    split = (pack_ref.shape[0], pack_ref.shape[2], units)
    pack_ref[:, 0, :, 0:units] = mm(xt_ref[...], gh_ref[...]).astype(BF).reshape(split)
    pack_ref[:, 0, :, units : 2 * units] = mm(gt_ref[...], act_ref[...]).astype(BF).reshape(split)

    @pl.when(pl.program_id(0) == pl.num_programs(0) - 1)
    def _():
        def one(r, carry):
            rows = pl.ds(pl.multiple_of(r * CHUNK, CHUNK), CHUNK)
            grad = direct_ref[rows, :] + back_ref[rows, :]
            hat = hat_ref[rows, :]
            summed = norm_backward(grad, hat, inverse_ref[rows, 0:1], vector_ref[1:2, :])
            summed_ref[rows, :] = summed
            summed_low_ref[rows, :] = summed.astype(BF)
            for i, value in enumerate((summed, grad * hat, grad)):
                total_ref[i : i + 1, :] += jnp.sum(value, axis=0, keepdims=True)
            return carry

        lax.fori_loop(0, x_ref.shape[0] // CHUNK, one, 0)


def feed_forward_backward(grad, x, act, slope, weights, direct, hat, inverse, vectors):
    length, features = x.shape
    dp, parts, cut, width = weights.shape
    units = act.shape[1] // parts
    piece = (dp, 1, cut, units)
    whole = once((length, features), (0, 0))
    rows = pl.BlockSpec((length, features), lambda t: (0, 0))
    part = pl.BlockSpec((length, units), lambda t: (0, t))
    return pl.pallas_call(
        feed_forward_backward_kernel,
        name="feed_forward_backward",
        out_shape=(
            jax.ShapeDtypeStruct((dp, parts, cut, width), BF),
            jax.ShapeDtypeStruct((parts, 1, units), F32),
            jax.ShapeDtypeStruct((length, features), F32),
            jax.ShapeDtypeStruct((length, features), BF),
            jax.ShapeDtypeStruct((8, features), F32),
        ),
        grid=(parts,),
        in_specs=[
            whole,
            whole,
            part,
            part,
            pl.BlockSpec(piece, lambda t: (0, t, 0, 0)),
            pl.BlockSpec(piece, lambda t: (0, t, 0, 1)),
            whole,
            whole,
            once((length, PAIR), (0, 0)),
            once((8, features), (0, 0)),
        ],
        out_specs=(
            pl.BlockSpec((dp, 1, cut, 2 * units), lambda t: (0, t, 0, 0)),
            pl.BlockSpec((1, 1, units), lambda t: (t, 0, 0)),
            rows,
            rows,
            pl.BlockSpec((8, features), lambda t: (0, 0)),
        ),
        scratch_shapes=[
            pltpu.VMEM((length, features), F32),
            pltpu.VMEM((features, length), BF),
            pltpu.VMEM((features, length), BF),
            pltpu.VMEM((length, units), BF),
        ],
        cost_estimate=pl.CostEstimate(
            flops=8 * length * features * parts * units,
            transcendentals=0,
            bytes_accessed=length * (parts * units * 4 + features * 18) + dp * parts * cut * width * 4,
        ),
        compiler_params=pltpu.CompilerParams(dimension_semantics=("arbitrary",)),
    )(grad, x, act, slope, weights, weights, direct, hat, inverse, vectors)


def output_gradient_kernel(
    spot_ref, grad_ref, kept_ref, got_ref, out_w_ref, _, pack_ref, own_ref, other_ref, full_ref, w_ref
):
    part = pl.program_id(0)
    columns = kept_ref.shape[1] // 2

    @pl.when(part == 0)
    def _():
        turned = grad_ref[...].T
        rest = jnp.zeros((turned.shape[0], 2 * PAIR - columns), F32)
        for k, ref in enumerate((kept_ref, got_ref)):
            result = mm(turned, ref[...])
            for x in range(2):
                piece = result[:, x * columns : (x + 1) * columns]
                full_ref[2 * k + x] = jnp.concatenate([piece, rest], axis=1).astype(BF)
        output_weights(out_w_ref, spot_ref, w_ref)
        own_ref[...] = mm(grad_ref[...], w_ref[0]).astype(BF)
        other_ref[...] = mm(grad_ref[...], w_ref[1]).astype(BF)

    other = (part % 2 + spot_ref[1]) % 2
    piece = full_ref[2 * other + part // 2]
    pack_ref[:, 0] = piece.reshape(pack_ref.shape[0], pack_ref.shape[2], pack_ref.shape[3])


def output_gradient(spot, grad, kept, got, weights, pack):
    length, features = grad.shape
    dp, parts, cut, width = pack.shape
    half = kept.shape[1]
    last = width // (2 * PAIR) - 1
    halves = pl.BlockSpec((length, half), lambda t, *_: (0, 0))
    return pl.pallas_call(
        output_gradient_kernel,
        name="output_gradient",
        out_shape=(
            jax.ShapeDtypeStruct(pack.shape, BF),
            jax.ShapeDtypeStruct((length, half), BF),
            jax.ShapeDtypeStruct((length, half), BF),
        ),
        grid_spec=pltpu.PrefetchScalarGridSpec(
            num_scalar_prefetch=1,
            grid=(parts,),
            in_specs=[
                once((length, features), (0, 0)),
                once((length, half), (0, 0)),
                once((length, half), (0, 0)),
                once((dp, parts, cut, 2 * PAIR), (0, 0, 0, last)),
                pl.BlockSpec(memory_space=pl.ANY),
            ],
            out_specs=(pl.BlockSpec((dp, 1, cut, 2 * PAIR), lambda t, *_: (0, t, 0, last)), halves, halves),
            scratch_shapes=[pltpu.VMEM((4, features, 2 * PAIR), BF), pltpu.VMEM((2, features, half), BF)],
        ),
        input_output_aliases={5: 0},
        cost_estimate=pl.CostEstimate(
            flops=4 * length * features * features, transcendentals=0, bytes_accessed=length * features * 8
        ),
        compiler_params=pltpu.CompilerParams(dimension_semantics=("arbitrary",)),
    )(spot, grad, kept, got, weights, pack)


def small_turns(bits):
    return [0, bits] + list(reversed(range(1, bits)))


def tiny_turns(bits):
    return list(range(1, bits)) + [0, bits]


def make_per_device(dp):
    bits = dp.bit_length() - 1
    assert dp == 1 << bits

    def per_device(
        tokens,
        segment_ids,
        w_query,
        w_key,
        w_value,
        w_out,
        b_query,
        b_value,
        w_up,
        w_down,
        b_up,
        b_out,
        gain_one,
        shift_one,
        b_down,
        gain_two,
        shift_two,
        cotangent,
    ):
        place = lax.axis_index("tensor")
        depth = lax.axis_index("dp")
        across = place // 2
        core = place % 2
        _, quarter, features = tokens.shape
        cut, columns = w_query.shape
        units = w_up.shape[1]
        half = 2 * columns
        pairs = half // PAIR
        first_core = core == 0
        first_chip = across == 0
        tiled = cut % 16 == 0

        def swap_chips(value):
            return lax.ppermute(value, "tensor", [(0, 2), (2, 0), (1, 3), (3, 1)])

        def swap_cores(value):
            return lax.ppermute(value, "tensor", [(0, 1), (1, 0), (2, 3), (3, 2)])

        def swap_bit(value, b):
            return lax.ppermute(value, "dp", [(i, i ^ (1 << b)) for i in range(dp)])

        def bit_of(b):
            return (depth >> b) & 1

        def in_order(flag, mine, other, axis):
            return jnp.stack([jnp.where(flag, mine, other), jnp.where(flag, other, mine)], axis=axis)

        def mine_of(value, index, axis):
            return lax.dynamic_index_in_dim(value, index, axis, keepdims=False)

        attention_pack = jnp.concatenate([w_query, w_key, w_value], axis=1)
        if tiled:
            gathered = jnp.stack([attention_pack, swap_chips(attention_pack)])
            for b in reversed(range(bits)):
                before_last = gathered
                gathered = jnp.concatenate([gathered, swap_bit(gathered, b)])
            spot = jnp.stack([depth, across]).astype(jnp.int32)
        else:
            gathered = lax.all_gather(attention_pack, BOTH, axis=0).reshape(dp, 2, 2, cut, 3 * columns)
            gathered = mine_of(gathered, core, 2).transpose(1, 0, 2, 3).reshape(2, dp * cut, 3 * columns)
            spot = jnp.zeros((2,), jnp.int32)

        tokens_own = in_order(first_chip, mine_of(tokens, across, 0), swap_chips(mine_of(tokens, 1 - across, 0)), 0)
        tokens_full = in_order(first_core, tokens_own, swap_cores(tokens_own), 1).reshape(4 * quarter, features)
        tokens_own = tokens_own.reshape(2 * quarter, features)

        small = [b_query, b_value, b_up, b_out, gain_one, shift_one, b_down, gain_two, shift_two]
        sizes = [v.size for v in small]
        lanes = -(-sum(sizes) // PAIR) * PAIR
        packed = jnp.concatenate([v.reshape(-1) for v in small])
        small_all = jnp.pad(packed, (0, lanes - packed.size)).reshape(1, lanes)
        turns = small_turns(bits)
        for b in turns:
            if b == bits:
                small_all = in_order(first_chip, small_all, swap_chips(small_all), 0)
            else:
                small_all = in_order(bit_of(b) == 0, small_all, swap_bit(small_all, b), 0)
        axes = turns[::-1]
        where = [axes.index(b) for b in reversed(range(bits))] + [axes.index(bits)]
        small_all = small_all.transpose(*where, bits + 1, bits + 2).reshape(dp, 2, 1, lanes)
        core_bias = small_all[:, :, 0, : sizes[0] + sizes[1]].reshape(dp, 2, 2, *b_query.shape).astype(F32)
        core_bias = core_bias.transpose(2, 1, 3, 0, 4).reshape(2, pairs, PAIR)
        bias_mine = jnp.stack([core_bias[0], jnp.zeros((pairs, PAIR), F32), core_bias[1]], axis=1).reshape(1, 3 * half)
        small_all = in_order(first_core, small_all, swap_cores(small_all), 2).reshape(dp, 4, lanes)
        pieces = []
        offset = 0
        for v, size in zip(small, sizes):
            piece = small_all[:, :, offset : offset + size].astype(F32)
            offset += size
            if v.ndim == 2:
                pieces.append(piece.reshape(dp, 4, *v.shape).transpose(1, 2, 0, 3))
            else:
                pieces.append(piece.reshape(-1))
        _, _, bias_up, out_bias, gain1, shift1, down_bias, gain2, shift2 = pieces
        bias_up = bias_up.reshape(4, 1, units)

        spare = jnp.zeros((cut, 2 * PAIR - columns), BF)
        other_pack = jnp.concatenate([w_up, w_down.T, w_out.T, spare], axis=1)
        width = other_pack.shape[1]
        if tiled:
            other_pack, _ = lax.optimization_barrier((other_pack, before_last))
        others = lax.all_gather(other_pack, BOTH, axis=0).reshape(dp, 4, cut, width)
        if not tiled:
            others = others.transpose(1, 0, 2, 3).reshape(1, 4, dp * cut, width)

        cotangent_sent = mine_of(cotangent, 1 - across, 0).astype(BF)
        cotangent_own = in_order(
            first_chip,
            mine_of(cotangent, across, 0),
            swap_chips(cotangent_sent).astype(F32),
            0,
        ).reshape(2 * quarter, features)
        segments = segment_bounds(mine_of(segment_ids, across, 0))

        *operands, w_qkv, limits = project(tokens_full, gathered, bias_mine, spot, *segments[3:])
        turn = jnp.stack([across, core]).astype(jnp.int32)
        kept, sent, lse = attention_forward(operands, limits, segments, turn)

        got = swap_cores(sent)
        flat = (2 * quarter, half)
        vectors = jnp.stack([out_bias, gain1, shift1, down_bias, gain2, shift2, out_bias, out_bias])
        activated, slope, hat1, inverse1, normed_low, out_keep, out_send, grad_z, grad_branch, totals2 = feed_forward(
            turn, kept.reshape(flat), got.reshape(flat), tokens_own, cotangent_own, vectors, others, bias_up
        )
        layer_out = in_order(first_chip, out_keep, swap_chips(out_send).astype(F32), 0)

        pack, grad_bias_up, grad_summed, grad_attended, totals1 = feed_forward_backward(
            grad_branch, normed_low, activated, slope, others, grad_z, hat1, inverse1, vectors
        )
        pack, grad_kept, grad_sent = output_gradient(
            turn, grad_attended, kept.reshape(flat), got.reshape(flat), others, pack
        )
        if not tiled:
            pack = pack.reshape(4, dp, cut, width).transpose(1, 0, 2, 3)
        others_mine = lax.psum_scatter(pack.reshape(4 * dp, cut, width), BOTH, scatter_dimension=0, tiled=False)

        grad_got = swap_cores(grad_sent.reshape(2, quarter, half))
        grads = (grad_kept.reshape(2, quarter, half), grad_got)
        grad_qkv = attention_backward(operands, grads, (kept, sent), lse, limits, segments, turn)
        part = mm_nt(grad_qkv, w_qkv).reshape(2, 2, quarter, features)
        part_kept = mine_of(part, core, 1)
        part_got = swap_cores(mine_of(part, 1 - core, 1).astype(BF))

        def send_back(value):
            kept_part = mine_of(value, across, 0)
            got_part = swap_chips(mine_of(value, 1 - across, 0).astype(BF)).astype(F32)
            return in_order(first_chip, kept_part, got_part, 0)

        grad_tokens = send_back(grad_summed.reshape(2, quarter, features) + part_kept + part_got.astype(F32))

        def halve(value, flag, swap, axis, kind):
            kept_half = mine_of(value, flag, axis)
            sent_half = mine_of(value, 1 - flag, axis)
            return (kept_half.astype(F32) + swap(sent_half).astype(F32)).astype(kind)

        grad_w = mm_tn(tokens_full, grad_qkv).astype(BF).reshape(dp, cut, 3 * half)
        for b in range(bits):
            grad_w = halve(grad_w.reshape(-1, 2, cut, 3 * half), bit_of(b), lambda v: swap_bit(v, b), 1, BF)
        grad_w = (
            grad_w.reshape(cut, pairs, 3, PAIR).transpose(0, 2, 1, 3).reshape(cut, 3, 2, columns).transpose(2, 0, 1, 3)
        )
        grad_w = halve(grad_w.reshape(2, cut, 3 * columns), across, lambda v: swap_chips(v), 0, F32)

        bias_grads = jnp.sum(grad_qkv.astype(F32), axis=0).reshape(pairs, 3, PAIR)

        def matrix_small(value, like):
            return value.reshape(2, 2, like.shape[0], dp, like.shape[1]).transpose(3, 0, 1, 2, 4).reshape(dp, 2, 2, -1)

        def head_small(value, like):
            value = value.reshape(2, columns)
            zero = jnp.zeros_like(value)
            both = [jnp.where(first_core, value, zero), jnp.where(first_core, zero, value)]
            return matrix_small(jnp.stack(both, axis=1), like)

        def vector_small(value):
            return value.reshape(dp, 2, 2, -1)

        small_grads = jnp.concatenate(
            [
                head_small(bias_grads[:, 0], b_query),
                head_small(bias_grads[:, 2], b_value),
                matrix_small(grad_bias_up, b_up),
                vector_small(totals1[0]),
                vector_small(totals1[1]),
                vector_small(totals1[2]),
                vector_small(totals2[0]),
                vector_small(totals2[1]),
                vector_small(totals2[2]),
            ],
            axis=3,
        )
        small_grads = jnp.pad(small_grads, ((0, 0), (0, 0), (0, 0), (0, lanes - small_grads.shape[3])))
        small_grads = halve(small_grads, core, lambda v: swap_cores(v), 2, F32)
        small_grads = small_grads.reshape((2,) * (bits + 1) + (lanes,))
        left = list(reversed(range(bits))) + [bits]
        for b in tiny_turns(bits):
            if b == bits:
                small_grads = halve(small_grads, across, lambda v: swap_chips(v), left.index(b), F32)
            else:
                small_grads = halve(small_grads, bit_of(b), lambda v: swap_bit(v, b), left.index(b), F32)
            left.remove(b)

        others_mine = others_mine.astype(F32)
        small_out = []
        offset = 0
        for v, size in zip(small, sizes):
            small_out.append(small_grads[offset : offset + size].reshape(v.shape))
            offset += size
        return (
            layer_out,
            grad_tokens,
            grad_w[:, :columns],
            grad_w[:, columns : 2 * columns],
            grad_w[:, 2 * columns :],
            others_mine[:, 2 * units : 2 * units + columns].T,
            small_out[0],
            small_out[1],
            others_mine[:, :units],
            others_mine[:, units : 2 * units].T,
            small_out[2],
            small_out[3],
            small_out[4],
            small_out[5],
            small_out[6],
            small_out[7],
            small_out[8],
        )

    return per_device


def solution(mesh):
    rows = P("dp", "tensor", None)
    split = P("dp", "tensor")
    turned = P("tensor", "dp")
    vector = P(("dp", "tensor"))
    in_specs = (rows, P("dp", None), split, split, split, turned, turned, turned, split, turned, turned)
    in_specs += (vector,) * 6 + (rows,)
    out_specs = (rows, rows, split, split, split, turned, turned, turned, split, turned, turned)
    out_specs += (vector,) * 6
    dp = mesh.shape["dp"]
    inner = make_per_device(dp)

    return jax.shard_map(inner, mesh=mesh, in_specs=in_specs, out_specs=out_specs, check_vma=False)
```
